256 devices in a mesh: head: 8 (over y, core), tok: 32 (over x, z).
Axes of the slice: x: 4, y: 4, z: 8, core: 2. Of those that a mesh axis runs over, the one named last changes fastest.
Arguments:
- hires_tokens: bfloat16 [131072, 1024], P('tok'), may hold values from -6 to 6
- lowres_tokens: bfloat16 [8192, 1024], P('tok'), may hold values from -6 to 6
- norm_gain: float32 [1024], replicated, may hold values from 0.1 to 1.9
- w_cross_q: bfloat16 [1024, 1024], P(None, 'head'), may hold values from -0.1875 to 0.1875
- w_low_kv: bfloat16 [1024, 2, 1024], P(None, None, 'head'), may hold values from -0.1875 to 0.1875
- w_view_qkv: bfloat16 [1024, 3, 1024], P(None, None, 'head'), may hold values from -0.1875 to 0.1875
- w_out: bfloat16 [2, 1024, 1024], P(None, 'head'), may hold values from -0.125 to 0.125
- block_lists: int32 [1024, 8], P('tok'), may hold values from 0 to 63, as said below
- block_counts: int32 [1024], P('tok'), may hold values from 1 to 8, as said below
Outputs:
- layer_out: bfloat16 [131072, 1024], P('tok', 'head')
The draws below stay inside these ranges and needn't reach their ends.
Inputs may be any that keep to these rules, and one draw needn't show every extreme that they name: `block_lists`: each row names 8 distinct low-resolution blocks; only the first block_counts entries of a row are used. `block_counts`: in every draw there is at least one index of tok all of whose query blocks use all 8 entries; query blocks of the other indices may use any count from 1 to 8.
All inputs are finite; a program needn't handle non-finite values.
Results may differ from the reference program's by a relative error of at most 0.009.
Values may be sent and summed in bfloat16 or wider, within the bound.
A program may use at most 128 MiB of HBM per device.

```python
import math
import jax
import jax.numpy as jnp
from jax import lax

D = 1024
HEADS = 8
HD = 128
VIEWS = 8
BLOCK = 128
MAXB = 8
TOK_DEV = 4096
TOKENS = 131072
PIX = 16384
LOWTOK = 8192
LOWBLK = 64
QBLK = 1024
N_HEAD = 8


def draw_block_lists(key, part):
    row_keys = jax.random.split(jax.random.fold_in(key, 11), QBLK)

    def one_row(row_key):
        return jax.random.permutation(row_key, LOWBLK)[:MAXB]
    return jax.vmap(one_row)(row_keys).astype(jnp.int32)


def draw_block_counts(key, part):
    per_dev = TOK_DEV // BLOCK
    devices = QBLK // per_dev
    key_level, key_draw, key_full = jax.random.split(jax.random.fold_in(key, 23), 3)
    dev_level = jax.random.randint(key_level, (devices, 1), 1, MAXB + 1)
    raw_draw = jax.random.randint(key_draw, (devices, per_dev), 0, 1 << 20)
    counts = 1 + raw_draw % dev_level
    full_dev = jax.random.randint(key_full, (), 0, devices)
    counts = jnp.where(jnp.arange(devices)[:, None] == full_dev, MAXB, counts)
    return counts.reshape(QBLK).astype(jnp.int32)


def block_scale(rng, extent, shards, low, top_value):
    factor_of = 1.0
    for position, parts in shards:
        draws = jax.random.uniform(jax.random.fold_in(jax.random.fold_in(rng, 6), position), (parts,), jnp.float32, low / len(shards), top_value / len(shards))
        factor_of = factor_of * jnp.repeat(jnp.exp(draws), extent[position] // parts).reshape((-1,) + (1,) * (len(extent) - 1 - position))
    return factor_of


def normal_values(stream_key, extent, width, reach, shards=(), held_as=jnp.bfloat16):
    entries = jax.random.normal(stream_key, extent, jnp.float32) * width
    if len(shards) > 0:
        entries = block_scale(stream_key, extent, shards, -0.22, 0.18) * entries
    return jnp.clip(entries, min=-reach, max=reach).astype(held_as)


def setup_inputs(seed: int = 0) -> dict:
    key_of = jax.random.split(jax.random.key(seed), 10)
    hires_tokens = normal_values(key_of[0], (TOKENS, D), 1.0, 6.0, ((0, 32),))
    lowres_tokens = normal_values(key_of[1], (LOWTOK, D), 1.0, 6.0, ((0, 32),))
    norm_gain = jnp.clip(1.0 + 0.18 * jax.random.normal(key_of[2], (D,), jnp.float32), 0.1, 1.9)
    w_cross_q = normal_values(key_of[3], (D, D), D ** -0.5, 0.1875, ((1, 8),))
    w_low_kv = normal_values(key_of[4], (D, 2, D), D ** -0.5, 0.1875, ((2, 8),))
    w_view_qkv = normal_values(key_of[5], (D, 3, D), D ** -0.5, 0.1875, ((2, 8),))
    w_out = normal_values(key_of[6], (2, D, D), (2 * D) ** -0.5, 0.125, ((1, 8),))
    block_lists = draw_block_lists(jax.random.fold_in(key_of[9], 71), 0)
    block_counts = draw_block_counts(jax.random.fold_in(key_of[9], 71), 0)
    return dict(hires_tokens=hires_tokens, lowres_tokens=lowres_tokens, norm_gain=norm_gain, w_cross_q=w_cross_q, w_low_kv=w_low_kv, w_view_qkv=w_view_qkv, w_out=w_out, block_lists=block_lists, block_counts=block_counts)


def rms_rows(row_block, norm_gain):
    values = row_block.astype(jnp.float32)
    factor = lax.rsqrt(lax.optimization_barrier(jnp.mean(values * values, axis=-1, keepdims=True)) + 1e-06)
    return (values * factor * norm_gain.astype(jnp.float32)).astype(jnp.bfloat16)

def masked_softmax(scores, is_valid):
    exponent = jnp.where(is_valid, jnp.exp(scores), jnp.zeros_like(scores))
    return (exponent / lax.optimization_barrier(jnp.sum(exponent, axis=-1, keepdims=True))).astype(jnp.bfloat16)

def reference(hires_tokens, lowres_tokens, norm_gain, w_cross_q, w_low_kv, w_view_qkv, w_out, block_lists, block_counts):
    normed = rms_rows(hires_tokens, norm_gain)
    low_normed = rms_rows(lowres_tokens, norm_gain)
    cross_query = jnp.dot(normed, w_cross_q, preferred_element_type=jnp.float32).astype(jnp.bfloat16)
    low_kv = jnp.dot(low_normed, w_low_kv.reshape(D, 2 * D), preferred_element_type=jnp.float32).astype(jnp.bfloat16)
    low_blocks = low_kv.reshape(LOWBLK, BLOCK, 2, HEADS, HD)
    q_blocks = cross_query.reshape(QBLK, BLOCK, HEADS, HD)
    slot_of_key = jnp.arange(MAXB * BLOCK, dtype=jnp.int32) // BLOCK

    def attend(inputs):
        queries, block_ids, live_count = inputs
        picked = low_blocks[block_ids].reshape(MAXB * BLOCK, 2, HEADS, HD).astype(jnp.float32)
        scores = jnp.einsum('qhe,khe->hqk', queries.astype(jnp.float32), picked[:, 0]) / math.sqrt(HD)
        weights = masked_softmax(scores, (slot_of_key < live_count)[None, None, :])
        mixed_out = jnp.einsum('hqk,khe->qhe', weights.astype(jnp.float32), picked[:, 1])
        return mixed_out.astype(jnp.bfloat16)
    cross_out = lax.map(attend, (q_blocks, block_lists, block_counts)).reshape(TOKENS, D)
    view_qkv = jnp.dot(normed, w_view_qkv.reshape(D, 3 * D), preferred_element_type=jnp.float32).astype(jnp.bfloat16)
    view_qkv = view_qkv.reshape(VIEWS, PIX, 3, HEADS, HD).astype(jnp.float32)
    scores = jnp.einsum('vphe,uphe->phvu', view_qkv[:, :, 0], view_qkv[:, :, 1]) / math.sqrt(HD)
    weights = masked_softmax(scores, True)
    view_out = jnp.einsum('phvu,uphe->vphe', weights.astype(jnp.float32), view_qkv[:, :, 2])
    view_out = view_out.astype(jnp.bfloat16).reshape(TOKENS, D)
    group_cols = D // N_HEAD
    total_sum = jnp.zeros((TOKENS, D), jnp.float32)
    for group_index in range(N_HEAD):
        lower = group_index * group_cols
        upper = lower + group_cols
        group_term = jnp.dot(cross_out[:, lower:upper], w_out[0, lower:upper], preferred_element_type=jnp.float32)
        group_term = group_term + jnp.dot(view_out[:, lower:upper], w_out[1, lower:upper], preferred_element_type=jnp.float32)
        rounded = lax.optimization_barrier(group_term.astype(jnp.bfloat16))
        total_sum = total_sum + rounded.astype(jnp.float32)
    return (hires_tokens.astype(jnp.float32) + total_sum).astype(jnp.bfloat16)
```

```python
import functools
import math

import jax
import jax.numpy as jnp
from jax import lax
from jax.experimental import pallas as pl
from jax.experimental.pallas import tpu as pltpu
from jax.sharding import PartitionSpec as P

HD = 128
VIEWS = 8
MAXB = 8
NY, NZ = 4, 8
CH = 4
PIECE = 16
HEADS = 8
MASKED = -1e30
SCORE_SCALE = math.log2(math.e) / math.sqrt(HD)
MESH = pl.DeviceIdType.MESH
F32 = jnp.float32
BF16 = jnp.bfloat16
Z_ORDER = (0, -1, 1, -2, 2, -3, 3, -4)


def rms_rows(values, gain):
    factor = lax.rsqrt(jnp.mean(values * values, axis=-1, keepdims=True) + 1e-06)
    return (values * factor * gain).astype(BF16)


def dot_t(a, b):
    return lax.dot_general(a, b, (((1,), (1,)), ((), ())), preferred_element_type=F32)


def dot(a, b):
    return jnp.dot(a, b, preferred_element_type=F32)


def kernel(
    x_hbm, meta_hbm, low_ref, gain_ref, wq_ref, wlow_ref, wout_ref, out_hbm,
    xp, kv, qc, oc, part, pr, fa, fb, r1, r2, res, meta_v, meta_s,
    s_a, r_a, l_a, s_b, r_b, s_z, r_z, s_x, r_x, s_xf, r_xf,
    s_o, r_o, s_ret, r_ret, l_ret, s_m, r_m, l_m,
):
    t = lax.axis_index("tok")
    h = lax.axis_index("head")
    x, z = t // NZ, lax.rem(t, NZ)
    y, c = h // 2, lax.rem(h, 2)
    v, q4 = t // 4, lax.rem(t, 4)

    def view_dev(s):
        return {"head": h, "tok": lax.rem(v + s, VIEWS) * 4 + q4}

    def y_of(d):
        return lax.rem(y + d + NY, NY)

    def y_dev(d):
        return {"head": y_of(d) * 2 + c, "tok": t}

    def z_of(d):
        return lax.rem(z + d + NZ, NZ)

    def x_of(d):
        return lax.rem(x + d + 4, 4)

    partner = {"head": y * 2 + 1 - c, "tok": t}
    y_up, y_dn = y_dev(1), y_dev(-1)
    z_up = {"head": h, "tok": x * NZ + z_of(1)}
    z_dn = {"head": h, "tok": x * NZ + z_of(-1)}
    x_up = {"head": h, "tok": x_of(1) * NZ + z}
    x_dn = {"head": h, "tok": x_of(-1) * NZ + z}

    def remote(src, dst, ss, rs, dev):
        return pltpu.make_async_remote_copy(
            src_ref=src, dst_ref=dst, send_sem=ss, recv_sem=rs, device_id=dev, device_id_type=MESH
        )

    def wait_bytes(ref, sem):
        pltpu.make_async_copy(ref, ref, sem).wait()

    barrier = pltpu.get_barrier_semaphore()
    peers = [view_dev(s) for s in range(1, VIEWS)] + [partner, y_up, y_dn, z_up, z_dn]
    for dev in peers:
        pl.semaphore_signal(barrier, inc=1, device_id=dev, device_id_type=MESH)
    pl.semaphore_wait(barrier, len(peers))

    def rows_start(k):
        for s in range(1, VIEWS):
            remote(
                x_hbm.at[lax.rem(v + s, VIEWS), k, h], xp.at[k, h, VIEWS - s],
                s_a.at[k], r_a.at[k], view_dev(s),
            ).start()
        pltpu.make_async_copy(x_hbm.at[v, k], xp.at[k, :, 0], l_a.at[k]).start()

    def piece(k, d, other=False):
        return xp.at[k, y_of(d) * 2 + (1 - c if other else c), pl.ds(1, VIEWS - 1)]

    def half(k, d, part_index):
        return xp.at[k, y_of(d) * 2 + c, pl.ds(1, VIEWS - 1), :, pl.ds(part_index * 512, 512)]

    def share(k, slot, ref, dev):
        return remote(ref, ref, s_b.at[k, slot], r_b.at[k, slot], dev)

    def in_a(k):
        wait_bytes(piece(k, 0), r_a.at[k])
        share(k, 0, piece(k, 0), y_up).start()
        share(k, 1, piece(k, 0), y_dn).start()
        share(k, 4, piece(k, 0), partner).start()

    def in_b(k):
        wait_bytes(piece(k, -1), r_b.at[k, 0])
        share(k, 2, half(k, -1, 0), y_up).start()
        share(k, 5, piece(k, -1), partner).start()
        wait_bytes(piece(k, 1), r_b.at[k, 1])
        share(k, 3, half(k, 1, 1), y_dn).start()
        share(k, 6, piece(k, 1), partner).start()

    def in_c(k):
        wait_bytes(half(k, 2, 0), r_b.at[k, 2])
        wait_bytes(half(k, 2, 1), r_b.at[k, 3])
        share(k, 7, piece(k, 2), partner).start()

    def in_d(k):
        for slot, d in ((4, 0), (5, -1), (6, 1), (7, 2)):
            wait_bytes(piece(k, d, True), r_b.at[k, slot])
        wait_bytes(xp.at[k, :, 0], l_a.at[k])

    def in_sends(k):
        wait_bytes(piece(k, 0), s_a.at[k])
        for slot, ref in (
            (0, piece(k, 0)), (1, piece(k, 0)), (2, half(k, -1, 0)), (3, half(k, 1, 1)),
            (4, piece(k, 0)), (5, piece(k, -1)), (6, piece(k, 1)), (7, piece(k, 2)),
        ):
            wait_bytes(ref, s_b.at[k, slot])

    def kv_block(dx, dz):
        return kv.at[pl.ds((x_of(dx) * NZ + z_of(dz)) * 2, 2)]

    def kv_half(dx, dz, part_index):
        return kv.at[(x_of(dx) * NZ + z_of(dz)) * 2 + part_index]

    def kv_z(i, dz, dev):
        return remote(kv_block(0, dz), kv_block(0, dz), s_z.at[i], r_z.at[i], dev)

    def kv_x_start(i):
        ref = kv_block(0, Z_ORDER[i])
        remote(ref, ref, s_x.at[i, 0], r_x.at[i, 0], x_up).start()
        remote(ref, ref, s_x.at[i, 1], r_x.at[i, 1], x_dn).start()

    def kv_x_forward(i):
        dz = Z_ORDER[i]
        wait_bytes(kv_block(-1, dz), r_x.at[i, 0])
        ref = kv_half(-1, dz, 0)
        remote(ref, ref, s_xf.at[i, 0], r_xf.at[i, 0], x_up).start()
        wait_bytes(kv_block(1, dz), r_x.at[i, 1])
        ref = kv_half(1, dz, 1)
        remote(ref, ref, s_xf.at[i, 1], r_xf.at[i, 1], x_dn).start()

    def kv_z_step(i):
        dz = Z_ORDER[i]
        wait_bytes(kv_block(0, dz), r_z.at[i])
        if i + 2 < VIEWS:
            kv_z(i + 2, dz, z_up if dz < 0 else z_dn).start()
        kv_x_start(i)

    def kv_last():
        for i, dz in enumerate(Z_ORDER):
            wait_bytes(kv_half(2, dz, 0), r_xf.at[i, 0])
            wait_bytes(kv_half(2, dz, 1), r_xf.at[i, 1])

    def kv_sends():
        for i, dz in enumerate(Z_ORDER):
            if i:
                wait_bytes(kv_block(0, dz), s_z.at[i])
            for e in range(2):
                wait_bytes(kv_block(0, dz), s_x.at[i, e])
                wait_bytes(kv_half(0, dz, 0), s_xf.at[i, e])

    for s in range(1, VIEWS):
        remote(
            meta_hbm.at[lax.rem(v + s, VIEWS)], meta_v.at[VIEWS - s], s_m, r_m, view_dev(s)
        ).start()
    pltpu.make_async_copy(meta_hbm.at[v], meta_v.at[0], l_m).start()

    rows_start(0)
    low = rms_rows(low_ref[...].astype(F32), gain_ref[...])
    kv[pl.ds(t * 2, 2)] = dot(low, wlow_ref[...]).astype(BF16).reshape(2, HD, 2 * HD)
    kv_z(1, 0, z_up).start()
    kv_z(2, 0, z_dn).start()
    kv_x_start(0)
    rows_start(1)

    row = lax.broadcasted_iota(jnp.int32, (HD, HD), 0)
    col = lax.broadcasted_iota(jnp.int32, (HD, HD), 1)
    same_pixel = jnp.where(lax.rem(row, PIECE) == lax.rem(col, PIECE), 0.0, MASKED).astype(F32)

    def project(k):
        def body(r, carry):
            rows = xp[k, pl.ds(r * 2, 2)].reshape(2 * HD, HEADS * HD).astype(F32)
            both = dot(rms_rows(rows, gain_ref[...]), wq_ref[...])
            scaled = jnp.concatenate([both[:, : 2 * HD] * SCORE_SCALE, both[:, 2 * HD :]], axis=1)
            qc[pl.ds(r * 2, 2)] = scaled.astype(BF16).reshape(2, VIEWS, PIECE, 4 * HD)
            return carry

        lax.fori_loop(0, HEADS // 2, body, 0)

    def view_attend():
        def body(g, carry):
            rows = qc[g].reshape(HD, 4 * HD)
            scores = dot_t(rows[:, HD : 2 * HD], rows[:, 2 * HD : 3 * HD]) + same_pixel
            weights = jnp.exp2(scores - jnp.max(scores, axis=-1, keepdims=True))
            total = jnp.sum(weights, axis=-1, keepdims=True)
            mixed = dot(weights.astype(BF16), rows[:, 3 * HD :]) / total
            oc[:, pl.ds(g * PIECE, PIECE), HD:] = mixed.astype(BF16).reshape(VIEWS, PIECE, HD)
            return carry

        lax.fori_loop(0, HEADS, body, 0, unroll=2)

    def cross_attend(k, first, last):
        def body(s, carry):
            queries = qc[:, s, :, :HD].reshape(HD, HD)
            count = meta_s[s, 0, 4 * MAXB + k]
            scores, values = [], []
            for pair in range(MAXB // 2):
                ids = [meta_s[s, 0, k * MAXB + 2 * pair + e] for e in range(2)]
                keys = jnp.concatenate([kv[ids[e], :, :HD] for e in range(2)], axis=0)
                values.append(jnp.concatenate([kv[ids[e], :, HD:] for e in range(2)], axis=0))
                raw = dot_t(queries, keys)
                for e in range(2):
                    bias = jnp.where(2 * pair + e < count, 0.0, MASKED).astype(F32)
                    scores.append(raw[:, e * HD : (e + 1) * HD] + bias)
            top = functools.reduce(jnp.maximum, scores)
            top = jnp.max(top, axis=-1, keepdims=True)
            weights = [jnp.exp2(score - top) for score in scores]
            total = jnp.sum(functools.reduce(jnp.add, weights), axis=-1, keepdims=True)
            mixed = functools.reduce(
                jnp.add,
                [
                    dot(jnp.concatenate(weights[2 * p : 2 * p + 2], axis=1).astype(BF16), values[p])
                    for p in range(MAXB // 2)
                ],
            )
            oc[s, :, :HD] = (mixed / total).astype(BF16)
            return carry

        lax.fori_loop(first, last, body, 0)

    def out_project(k):
        def body(r, carry):
            rows = oc[pl.ds(r * 2, 2)].reshape(2 * HD, 2 * HD)
            summed = dot(rows, wout_ref[...]).astype(BF16)
            for j in range(HEADS):
                part[k, j % 2, j // 2, pl.ds(r * 2 * HD, 2 * HD)] = summed[:, j * HD : (j + 1) * HD]
            return carry

        lax.fori_loop(0, VIEWS // 2, body, 0)

    def core_send(k):
        return remote(part.at[k, 1 - c], pr.at[k], s_o.at[k, 0], r_o.at[k, 0], partner)

    def far_sends(k):
        a = y_of(2)
        return (
            remote(part.at[k, c, a, pl.ds(0, 512)], fa.at[k], s_o.at[k, 1], r_o.at[k, 1], y_up),
            remote(part.at[k, c, a, pl.ds(512, 512)], fb.at[k], s_o.at[k, 2], r_o.at[k, 2], y_dn),
        )

    def near_sends(k):
        return (
            remote(part.at[k, c, y_of(1)], r1.at[k], s_o.at[k, 3], r_o.at[k, 3], y_up),
            remote(part.at[k, c, y_of(-1)], r2.at[k], s_o.at[k, 4], r_o.at[k, 4], y_dn),
        )

    def out_a(k):
        core_send(k).wait_recv()
        a = y_of(2)

        def body(r, carry):
            rows = pl.ds(r * 256, 256)
            part[k, c, a, rows] = (part[k, c, a, rows].astype(F32) + pr[k, a, rows].astype(F32)).astype(BF16)
            return carry

        lax.fori_loop(0, 4, body, 0)
        for copy in far_sends(k):
            copy.start()

    def out_b(k):
        for copy in far_sends(k):
            copy.wait_recv()
        up, dn = y_of(1), y_of(-1)

        def body(r, carry):
            with_far, without = pl.ds(r * 256, 256), pl.ds(512 + r * 256, 256)
            for a, far, w0, w1 in ((up, fa, with_far, without), (dn, fb, without, with_far)):
                part[k, c, a, w0] = (
                    part[k, c, a, w0].astype(F32) + pr[k, a, w0].astype(F32)
                    + far[k, pl.ds(r * 256, 256)].astype(F32)
                ).astype(BF16)
                part[k, c, a, w1] = (part[k, c, a, w1].astype(F32) + pr[k, a, w1].astype(F32)).astype(BF16)
            return carry

        lax.fori_loop(0, 2, body, 0)
        for copy in near_sends(k):
            copy.start()

    def home(k, s):
        return remote(res.at[k, s], out_hbm.at[v, k], s_ret.at[k], r_ret.at[k], view_dev(s))

    def out_c(k):
        for copy in near_sends(k):
            copy.wait_recv()

        def body(s, carry):
            rows = pl.ds(s * HD, HD)
            total = part[k, c, y, rows].astype(F32) + pr[k, y, rows].astype(F32)
            total = total + r1[k, rows].astype(F32) + r2[k, rows].astype(F32)
            columns = pl.ds(pl.multiple_of(h * HD, HD), HD)
            residual = xp[k, :, s, :, columns].reshape(HD, HD).astype(F32)
            res[k, s] = (residual + total).astype(BF16)
            return carry

        lax.fori_loop(0, VIEWS, body, 0)
        for s in range(1, VIEWS):
            home(k, s).start()
        pltpu.make_async_copy(res.at[k, 0], out_hbm.at[v, k], l_ret.at[k]).start()

    def out_sends(k):
        for copy in (core_send(k),) + far_sends(k) + near_sends(k):
            copy.wait_send()
        wait_bytes(res.at[k, pl.ds(1, VIEWS - 1)], s_ret.at[k])
        wait_bytes(res.at[k, pl.ds(1, VIEWS - 1)], r_ret.at[k])
        wait_bytes(res.at[k, 0], l_ret.at[k])

    kv_z_step(1)
    kv_z_step(2)
    in_a(0)
    rows_start(2)
    kv_z_step(3)
    kv_z_step(4)
    kv_x_forward(0)
    in_b(0)
    rows_start(3)
    kv_z_step(5)
    kv_z_step(6)
    in_c(0)
    kv_z_step(7)
    wait_bytes(meta_v.at[pl.ds(1, VIEWS - 1)], r_m)
    wait_bytes(meta_v.at[0], l_m)
    meta_copy = pltpu.make_async_copy(meta_v, meta_s, l_m)
    meta_copy.start()
    for i in range(1, VIEWS):
        kv_x_forward(i)
    in_d(0)
    meta_copy.wait()

    def step(i, carry):
        kin, kc, ko = i, i - 1, i - 2
        has_in = jnp.logical_and(i > 0, i < CH)
        has_c = jnp.logical_and(i > 0, i <= CH)
        has_o = i > 1

        @pl.when(has_in)
        def _():
            in_a(kin)

        @pl.when(has_c)
        def _():
            project(kc)

        @pl.when(has_in)
        def _():
            in_b(kin)

        @pl.when(has_o)
        def _():
            out_a(ko)

        @pl.when(has_c)
        def _():
            view_attend()

            @pl.when(i == 1)
            def _():
                kv_last()

            cross_attend(kc, 0, 3)

        @pl.when(has_o)
        def _():
            out_b(ko)

        @pl.when(has_in)
        def _():
            in_c(kin)

        @pl.when(has_c)
        def _():
            cross_attend(kc, 3, VIEWS)

        @pl.when(has_o)
        def _():
            out_c(ko)

        @pl.when(has_c)
        def _():
            out_project(kc)
            core_send(kc).start()

        @pl.when(has_in)
        def _():
            in_d(kin)

        return carry

    lax.fori_loop(1, CH + 2, step, 0)

    wait_bytes(meta_v.at[pl.ds(1, VIEWS - 1)], s_m)
    kv_sends()

    def drain(k, carry):
        in_sends(k)
        out_sends(k)
        return carry

    lax.fori_loop(0, CH, drain, 0)


def shards(hires, low, gain, w_cross_q, w_low_kv, w_view_qkv, w_out, lists, counts):
    width = hires.shape[1]
    cols = w_cross_q.shape[1]
    rows = hires.reshape(VIEWS, CH, HEADS, PIECE, width)
    wq = jnp.concatenate([w_cross_q, w_view_qkv.reshape(width, 3 * cols)], axis=1)
    meta = jnp.concatenate([lists.reshape(VIEWS, CH * MAXB), counts.reshape(VIEWS, CH)], axis=1)
    meta = jnp.pad(meta[:, None, :], ((0, 0), (0, 7), (0, HD - CH * MAXB - CH)))
    vmem = pl.BlockSpec(memory_space=pltpu.VMEM)
    hbm = pl.BlockSpec(memory_space=pl.ANY)
    dma = pltpu.SemaphoreType.DMA
    out = pl.pallas_call(
        kernel,
        out_shape=jax.ShapeDtypeStruct((VIEWS, CH, HD, HD), BF16),
        in_specs=[hbm, hbm, vmem, vmem, vmem, vmem, vmem],
        out_specs=hbm,
        scratch_shapes=[
            pltpu.VMEM((CH, HEADS, VIEWS, PIECE, width), BF16),
            pltpu.VMEM((64, HD, 2 * HD), BF16),
            pltpu.VMEM((HEADS, VIEWS, PIECE, 4 * HD), BF16),
            pltpu.VMEM((VIEWS, HD, 2 * HD), BF16),
            pltpu.VMEM((CH, 2, NY, VIEWS * HD, HD), BF16),
            pltpu.VMEM((CH, NY, VIEWS * HD, HD), BF16),
            pltpu.VMEM((CH, 512, HD), BF16),
            pltpu.VMEM((CH, 512, HD), BF16),
            pltpu.VMEM((CH, VIEWS * HD, HD), BF16),
            pltpu.VMEM((CH, VIEWS * HD, HD), BF16),
            pltpu.VMEM((CH, VIEWS, HD, HD), BF16),
            pltpu.VMEM((VIEWS, 8, HD), jnp.int32),
            pltpu.SMEM((VIEWS, 8, HD), jnp.int32),
            dma((CH,)), dma((CH,)), dma((CH,)),
            dma((CH, 8)), dma((CH, 8)),
            dma((8,)), dma((8,)),
            dma((8, 2)), dma((8, 2)),
            dma((8, 2)), dma((8, 2)),
            dma((CH, 5)), dma((CH, 5)),
            dma((CH,)), dma((CH,)), dma((CH,)),
            dma, dma, dma,
        ],
        name="upscaler",
        compiler_params=pltpu.CompilerParams(
            collective_id=0, has_side_effects=True, vmem_limit_bytes=60 * 1024 * 1024
        ),
    )(rows, meta, low, gain.reshape(1, width), wq, w_low_kv.reshape(width, 2 * cols), w_out.reshape(2 * cols, width))
    return out.reshape(hires.shape[0], cols)


def solution(mesh):
    in_specs = (
        P("tok", None),
        P("tok", None),
        P(),
        P(None, "head"),
        P(None, None, "head"),
        P(None, None, "head"),
        P(None, "head", None),
        P("tok", None),
        P("tok"),
    )
    return jax.shard_map(shards, mesh=mesh, in_specs=in_specs, out_specs=P("tok", "head"), check_vma=False)
```

```python
import functools
import math

import jax
import jax.numpy as jnp
from jax import lax
from jax.experimental import pallas as pl
from jax.experimental.pallas import tpu as pltpu
from jax.sharding import PartitionSpec as P

HD = 128
VIEWS = 8
MAXB = 8
NY, NZ = 4, 8
CH = 4
PIECE = 16
HEADS = 8
MASKED = -1e30
SCORE_SCALE = math.log2(math.e) / math.sqrt(HD)
MESH = pl.DeviceIdType.MESH
F32 = jnp.float32
BF16 = jnp.bfloat16
Z_ORDER = (0, -1, 1, -2, 2, -3, 3, -4)
SLOT_VIEW = (0, 2, 4, 6, 1, 3, 5, 7)
GROUPS = ((1, 3), (4, 4))
KV_MAIN = 112


def rms_rows(values, gain):
    factor = lax.rsqrt(jnp.mean(values * values, axis=-1, keepdims=True) + 1e-06)
    return (values * factor * gain).astype(BF16)


def dot_t(a, b):
    return lax.dot_general(a, b, (((1,), (1,)), ((), ())), preferred_element_type=F32)


def dot(a, b):
    return jnp.dot(a, b, preferred_element_type=F32)


def kernel(
    x_hbm, meta_hbm, low_ref, gain_ref, wq_ref, wlow_ref, wout_ref, out_hbm,
    xp, kv, kvb, qc, oc, part, pr, fa, fb, r1, r2, res, meta_v, meta_s,
    s_a, r_a, l_a, s_b, r_b, s_z, r_z, s_x, r_x, s_xf, r_xf, s_h, r_h, s_hz, r_hz,
    s_o, r_o, s_ret, r_ret, l_ret, s_m, r_m, l_m,
):
    t = lax.axis_index("tok")
    h = lax.axis_index("head")
    x, z = t // NZ, lax.rem(t, NZ)
    y, c = h // 2, lax.rem(h, 2)
    v, q4 = t // 4, lax.rem(t, 4)

    def view_dev(s):
        return {"head": h, "tok": lax.rem(v + s, VIEWS) * 4 + q4}

    def y_of(d):
        return lax.rem(y + d + NY, NY)

    def y_dev(d):
        return {"head": y_of(d) * 2 + c, "tok": t}

    def z_of(d):
        return lax.rem(z + d + NZ, NZ)

    def x_of(d):
        return lax.rem(x + d + 4, 4)

    partner = {"head": y * 2 + 1 - c, "tok": t}
    y_up, y_dn = y_dev(1), y_dev(-1)
    z_up = {"head": h, "tok": x * NZ + z_of(1)}
    z_dn = {"head": h, "tok": x * NZ + z_of(-1)}
    x_up = {"head": h, "tok": x_of(1) * NZ + z}
    x_dn = {"head": h, "tok": x_of(-1) * NZ + z}

    def remote(src, dst, ss, rs, dev):
        return pltpu.make_async_remote_copy(
            src_ref=src, dst_ref=dst, send_sem=ss, recv_sem=rs, device_id=dev, device_id_type=MESH
        )

    def wait_bytes(ref, sem):
        pltpu.make_async_copy(ref, ref, sem).wait()

    barrier = pltpu.get_barrier_semaphore()
    peers = [view_dev(s) for s in range(1, VIEWS)] + [partner, y_up, y_dn, z_up, z_dn]
    for dev in peers:
        pl.semaphore_signal(barrier, inc=1, device_id=dev, device_id_type=MESH)
    pl.semaphore_wait(barrier, len(peers))

    def slot_of(s):
        return SLOT_VIEW.index(s % VIEWS)

    def slots(g):
        return pl.ds(*GROUPS[g])

    def rows_start(k, g):
        first, n = GROUPS[g]
        for s in SLOT_VIEW[first : first + n]:
            remote(
                x_hbm.at[lax.rem(v + s, VIEWS), k, h], xp.at[k, h, slot_of(-s)],
                s_a.at[k, g], r_a.at[k, g], view_dev(s),
            ).start()
        if g == 0:
            pltpu.make_async_copy(x_hbm.at[v, k], xp.at[k, :, 0], l_a.at[k]).start()

    def piece(k, g, d, other=False):
        return xp.at[k, y_of(d) * 2 + (1 - c if other else c), slots(g)]

    def share(k, g, slot, ref, dev):
        return remote(ref, ref, s_b.at[k, g, slot], r_b.at[k, g, slot], dev)

    def in_a(k, g):
        own = piece(k, g, 0)
        wait_bytes(own, r_a.at[k, g])
        share(k, g, 0, own, y_up).start()
        share(k, g, 1, own, y_dn).start()
        share(k, g, 3, own, partner).start()

    def in_b(k, g):
        wait_bytes(piece(k, g, -1), r_b.at[k, g, 0])
        if g == 0:
            share(k, g, 2, piece(k, g, -1), y_up).start()
        share(k, g, 4, piece(k, g, -1), partner).start()
        wait_bytes(piece(k, g, 1), r_b.at[k, g, 1])
        if g == 1:
            share(k, g, 2, piece(k, g, 1), y_dn).start()
        share(k, g, 5, piece(k, g, 1), partner).start()

    def in_c(k, g):
        wait_bytes(piece(k, g, 2), r_b.at[k, g, 2])
        share(k, g, 6, piece(k, g, 2), partner).start()

    def in_d(k):
        for g in range(2):
            for slot, d in ((3, 0), (4, -1), (5, 1), (6, 2)):
                wait_bytes(piece(k, g, d, True), r_b.at[k, g, slot])
        wait_bytes(xp.at[k, :, 0], l_a.at[k])

    def in_sends(k):
        for g in range(2):
            wait_bytes(piece(k, g, 0), s_a.at[k, g])
            for slot in range(7):
                wait_bytes(piece(k, g, 0), s_b.at[k, g, slot])

    def kv_block(dx, dz):
        return kv.at[pl.ds((x_of(dx) * NZ + z_of(dz)) * 2, 2)]

    def kv_half(dx, dz, part_index):
        return kv.at[(x_of(dx) * NZ + z_of(dz)) * 2 + part_index]

    def kv_z(i, dz, dev):
        return remote(kv_block(0, dz), kv_block(0, dz), s_z.at[i], r_z.at[i], dev)

    def kv_x_start(i):
        ref = kv_block(0, Z_ORDER[i])
        remote(ref, ref, s_x.at[i, 0], r_x.at[i, 0], x_up).start()
        remote(ref, ref, s_x.at[i, 1], r_x.at[i, 1], x_dn).start()

    def kv_x_forward(i):
        dz = Z_ORDER[i]
        wait_bytes(kv_block(-1, dz), r_x.at[i, 0])
        ref = kv_half(-1, dz, 0)
        remote(ref, ref, s_xf.at[i, 0], r_xf.at[i, 0], x_up).start()
        wait_bytes(kv_block(1, dz), r_x.at[i, 1])
        ref = kv_half(1, dz, 1)
        remote(ref, ref, s_xf.at[i, 1], r_xf.at[i, 1], x_dn).start()

    def kv_z_step(i):
        dz = Z_ORDER[i]
        wait_bytes(kv_block(0, dz), r_z.at[i])
        if i + 2 < VIEWS:
            kv_z(i + 2, dz, z_up if dz < 0 else z_dn).start()
        kv_x_start(i)

    def kvb_x_block(d):
        return kvb.at[pl.ds((z * 4 + x_of(d)) * 2, 2)]

    def kvb_x_half(d, e):
        return kvb.at[(z * 4 + x_of(d)) * 2 + e]

    def kvb_z_block(d):
        return kvb.at[pl.ds(z_of(d) * 8, 8)]

    def kvb_x():
        wait_bytes(kvb_x_block(-1), r_h.at[0])
        remote(kvb_x_half(-1, 0), kvb_x_half(-1, 0), s_h.at[2], r_h.at[2], x_up).start()
        wait_bytes(kvb_x_block(1), r_h.at[1])
        remote(kvb_x_half(1, 1), kvb_x_half(1, 1), s_h.at[3], r_h.at[3], x_dn).start()

    def kvb_z(i, dz, dev):
        return remote(kvb_z_block(dz), kvb_z_block(dz), s_hz.at[i], r_hz.at[i], dev)

    def kvb_xf():
        wait_bytes(kvb_x_half(2, 0), r_h.at[2])
        wait_bytes(kvb_x_half(2, 1), r_h.at[3])
        kvb_z(1, 0, z_up).start()
        kvb_z(2, 0, z_dn).start()

    def kvb_z_step(i):
        dz = Z_ORDER[i]
        wait_bytes(kvb_z_block(dz), r_hz.at[i])
        kvb_z(i + 2, dz, z_up if dz < 0 else z_dn).start()

    def kv_last():
        meta_in()
        for i in (6, 7):
            wait_bytes(kvb_z_block(Z_ORDER[i]), r_hz.at[i])
        for i, dz in enumerate(Z_ORDER):
            wait_bytes(kv_half(2, dz, 0), r_xf.at[i, 0])
            wait_bytes(kv_half(2, dz, 1), r_xf.at[i, 1])

    def kv_sends():
        for e in range(2):
            wait_bytes(kvb_x_block(0), s_h.at[e])
            wait_bytes(kvb_x_half(0, e), s_h.at[2 + e])
        for i in range(1, VIEWS):
            wait_bytes(kvb_z_block(0), s_hz.at[i])
        for i, dz in enumerate(Z_ORDER):
            if i:
                wait_bytes(kv_block(0, dz), s_z.at[i])
            for e in range(2):
                wait_bytes(kv_block(0, dz), s_x.at[i, e])
                wait_bytes(kv_half(0, dz, 0), s_xf.at[i, e])

    for s in range(1, VIEWS):
        remote(
            meta_hbm.at[lax.rem(v + s, VIEWS)], meta_v.at[slot_of(-s)], s_m, r_m, view_dev(s)
        ).start()
    pltpu.make_async_copy(meta_hbm.at[v], meta_v.at[0], l_m).start()

    def low_start():
        low = rms_rows(low_ref[...].astype(F32), gain_ref[...])
        both = dot(low, wlow_ref[...]).astype(BF16).reshape(2, HD, 2 * HD)
        kv[pl.ds(t * 2, 2)] = both[:, :KV_MAIN]
        kvb[pl.ds((z * 4 + x) * 2, 2)] = both[:, KV_MAIN:]
        kv_z(1, 0, z_up).start()
        kv_z(2, 0, z_dn).start()
        for e, dev in ((0, x_up), (1, x_dn)):
            remote(kvb_x_block(0), kvb_x_block(0), s_h.at[e], r_h.at[e], dev).start()
        kv_x_start(0)

    row = lax.broadcasted_iota(jnp.int32, (HD, HD), 0)
    col = lax.broadcasted_iota(jnp.int32, (HD, HD), 1)
    same_pixel = jnp.where(lax.rem(row, PIECE) == lax.rem(col, PIECE), 0.0, MASKED).astype(F32)

    def project(k):
        def body(r, carry):
            rows = xp[k, pl.ds(r * 2, 2)].reshape(2 * HD, HEADS * HD).astype(F32)
            both = dot(rms_rows(rows, gain_ref[...]), wq_ref[...])
            scaled = jnp.concatenate([both[:, : 2 * HD] * SCORE_SCALE, both[:, 2 * HD :]], axis=1)
            qc[k, pl.ds(r * 2, 2)] = scaled.astype(BF16).reshape(2, VIEWS, PIECE, 4 * HD)
            return carry

        lax.fori_loop(0, HEADS // 2, body, 0)

    def view_attend(k):
        def body(g, carry):
            rows = qc[k, g].reshape(HD, 4 * HD)
            scores = dot_t(rows[:, HD : 2 * HD], rows[:, 2 * HD : 3 * HD]) + same_pixel
            weights = jnp.exp2(scores - jnp.max(scores, axis=-1, keepdims=True))
            total = jnp.sum(weights, axis=-1, keepdims=True)
            mixed = dot(weights.astype(BF16), rows[:, 3 * HD :]) / total
            oc[k, :, pl.ds(g * PIECE, PIECE), HD:] = mixed.astype(BF16).reshape(VIEWS, PIECE, HD)
            return carry

        lax.fori_loop(0, HEADS, body, 0, unroll=2)

    def cross_attend(k, u):
        def body(i, carry):
            s = u * 4 + i
            queries = qc[k, :, s, :, :HD].reshape(HD, HD)
            count = meta_s[s, 0, 2 * CH * MAXB + k]
            scores, values = [], []
            for pair in range(MAXB // 2):
                blocks = []
                for e in range(2):
                    at = k * MAXB + 2 * pair + e
                    blocks += [kv[meta_s[s, 0, at]], kvb[meta_s[s, 0, CH * MAXB + at]]]
                both = jnp.concatenate(blocks, axis=0)
                keys = both[:, :HD]
                values.append(both[:, HD:])
                raw = dot_t(queries, keys)
                for e in range(2):
                    bias = jnp.where(2 * pair + e < count, 0.0, MASKED).astype(F32)
                    scores.append(raw[:, e * HD : (e + 1) * HD] + bias)
            top = functools.reduce(jnp.maximum, scores)
            top = jnp.max(top, axis=-1, keepdims=True)
            weights = [jnp.exp2(score - top) for score in scores]
            total = jnp.sum(functools.reduce(jnp.add, weights), axis=-1, keepdims=True)
            mixed = functools.reduce(
                jnp.add,
                [
                    dot(jnp.concatenate(weights[2 * p : 2 * p + 2], axis=1).astype(BF16), values[p])
                    for p in range(MAXB // 2)
                ],
            )
            oc[k, s, :, :HD] = (mixed / total).astype(BF16)
            return carry

        lax.fori_loop(0, 4, body, 0)

    def out_project(k, u):
        def body(r, carry):
            rows = oc[k, pl.ds(u * 4 + r * 2, 2)].reshape(2 * HD, 2 * HD)
            summed = dot(rows, wout_ref[...]).astype(BF16)
            for j in range(HEADS):
                part[k, u, j % 2, j // 2, pl.ds(r * 2 * HD, 2 * HD)] = summed[:, j * HD : (j + 1) * HD]
            return carry

        lax.fori_loop(0, 2, body, 0)
        core_send(k, u).start()

    def core_send(k, u):
        return remote(part.at[k, u, 1 - c], pr.at[k, u], s_o.at[k, u, 0], r_o.at[k, u, 0], partner)

    def far_sends(k, u):
        a = y_of(2)
        return (
            remote(part.at[k, u, c, a, pl.ds(0, 256)], fa.at[k, u], s_o.at[k, u, 1], r_o.at[k, u, 1], y_up),
            remote(part.at[k, u, c, a, pl.ds(256, 256)], fb.at[k, u], s_o.at[k, u, 2], r_o.at[k, u, 2], y_dn),
        )

    def near_sends(k, u):
        return (
            remote(part.at[k, u, c, y_of(1)], r1.at[k, u], s_o.at[k, u, 3], r_o.at[k, u, 3], y_up),
            remote(part.at[k, u, c, y_of(-1)], r2.at[k, u], s_o.at[k, u, 4], r_o.at[k, u, 4], y_dn),
        )

    def add_core(k, u, a, rows):
        return part[k, u, c, a, rows].astype(F32) + pr[k, u, a, rows].astype(F32)

    def out_a(k, u):
        core_send(k, u).wait_recv()
        a = y_of(2)

        def body(r, carry):
            rows = pl.ds(r * 256, 256)
            part[k, u, c, a, rows] = add_core(k, u, a, rows).astype(BF16)
            return carry

        lax.fori_loop(0, 2, body, 0)
        for copy in far_sends(k, u):
            copy.start()

    def out_b(k, u):
        for copy in far_sends(k, u):
            copy.wait_recv()
        up, dn = y_of(1), y_of(-1)

        def body(r, carry):
            w, first, second = pl.ds(r * 128, 128), pl.ds(r * 128, 128), pl.ds(256 + r * 128, 128)
            for a, far, with_far, without in ((up, fa, first, second), (dn, fb, second, first)):
                part[k, u, c, a, with_far] = (add_core(k, u, a, with_far) + far[k, u, w].astype(F32)).astype(BF16)
                part[k, u, c, a, without] = add_core(k, u, a, without).astype(BF16)
            return carry

        lax.fori_loop(0, 2, body, 0)
        for copy in near_sends(k, u):
            copy.start()

    def home_slots(u):
        return range(1, 4) if u == 0 else range(4, VIEWS)

    def home(k, u, p):
        return remote(
            res.at[k, p], out_hbm.at[v, k], s_ret.at[k, u], r_ret.at[k, u], view_dev(SLOT_VIEW[p])
        )

    def out_c(k, u):
        for copy in near_sends(k, u):
            copy.wait_recv()

        def body(i, carry):
            p = u * 4 + i
            rows = pl.ds(i * HD, HD)
            total = add_core(k, u, y, rows) + r1[k, u, rows].astype(F32) + r2[k, u, rows].astype(F32)
            columns = pl.ds(pl.multiple_of(h * HD, HD), HD)
            residual = xp[k, :, p, :, columns].reshape(HD, HD).astype(F32)
            res[k, p] = (residual + total).astype(BF16)
            return carry

        lax.fori_loop(0, 4, body, 0)
        for p in home_slots(u):
            home(k, u, p).start()
        if u == 0:
            pltpu.make_async_copy(res.at[k, 0], out_hbm.at[v, k], l_ret.at[k]).start()

    def out_sends(k):
        for u in range(2):
            for copy in (core_send(k, u),) + far_sends(k, u) + near_sends(k, u):
                copy.wait_send()
            sent = res.at[k, slots(u)]
            wait_bytes(sent, s_ret.at[k, u])
            wait_bytes(sent, r_ret.at[k, u])
        wait_bytes(res.at[k, 0], l_ret.at[k])

    meta_copy = pltpu.make_async_copy(meta_v, meta_s, l_m)

    def meta_in():
        wait_bytes(meta_v.at[pl.ds(1, VIEWS - 1)], r_m)
        wait_bytes(meta_v.at[0], l_m)
        meta_copy.start()
        meta_copy.wait()

    rows_start(0, 1)
    rows_start(3, 0)
    rows_start(2, 0)
    rows_start(0, 0)
    low_start()
    in_a(2, 0)
    in_a(3, 0)
    kvb_x()
    rows_start(2, 1)
    in_a(0, 1)
    rows_start(1, 0)
    kv_z_step(1)
    kv_z_step(2)
    kvb_xf()
    kv_x_forward(0)
    in_a(0, 0)
    rows_start(3, 1)
    in_b(2, 0)
    in_b(0, 1)
    in_a(2, 1)
    kv_z_step(3)
    kv_x_forward(1)
    in_c(0, 1)
    in_a(1, 0)
    kv_x_forward(2)
    in_b(2, 1)
    in_b(0, 0)
    kvb_z_step(1)
    kv_z_step(4)
    kvb_z_step(2)
    in_b(3, 0)
    kv_x_forward(3)
    in_a(3, 1)
    kv_z_step(5)
    in_c(2, 1)
    kv_z_step(6)
    in_c(2, 0)
    rows_start(1, 1)
    kv_x_forward(4)
    in_c(0, 0)
    in_d(2)
    project(2)
    kv_z_step(7)
    in_b(3, 1)
    kvb_z_step(3)
    in_b(1, 0)
    view_attend(2)
    kvb_z_step(4)
    kv_x_forward(5)
    in_c(3, 1)
    kv_x_forward(6)
    in_d(0)
    project(0)
    in_c(3, 0)
    kv_x_forward(7)
    in_c(1, 0)
    kvb_z_step(5)
    in_a(1, 1)
    view_attend(0)
    in_d(3)
    project(3)
    kv_last()
    cross_attend(2, 0)
    out_project(2, 0)
    in_b(1, 1)
    cross_attend(0, 1)
    out_project(0, 1)
    view_attend(3)
    out_a(2, 0)
    cross_attend(2, 1)
    out_a(0, 1)
    out_project(2, 1)
    cross_attend(3, 1)
    out_b(2, 0)
    in_c(1, 1)
    out_project(3, 1)
    out_a(2, 1)
    out_b(0, 1)
    in_d(1)
    project(1)
    view_attend(1)
    out_a(3, 1)
    cross_attend(1, 0)
    cross_attend(3, 0)
    out_b(2, 1)
    out_project(3, 0)
    out_c(0, 1)
    cross_attend(0, 0)
    out_b(3, 1)
    out_project(1, 0)
    out_a(3, 0)
    out_project(0, 0)
    cross_attend(1, 1)
    out_a(1, 0)
    out_project(1, 1)
    out_c(2, 1)
    out_c(3, 1)
    out_a(0, 0)
    out_c(2, 0)
    out_a(1, 1)
    out_b(1, 0)
    out_b(1, 1)
    out_b(0, 0)
    out_b(3, 0)
    out_c(1, 0)
    out_c(1, 1)
    out_c(0, 0)
    out_c(3, 0)

    wait_bytes(meta_v.at[pl.ds(1, VIEWS - 1)], s_m)
    kv_sends()

    def drain(k, carry):
        in_sends(k)
        out_sends(k)
        return carry

    lax.fori_loop(0, CH, drain, 0)


def shards(hires, low, gain, w_cross_q, w_low_kv, w_view_qkv, w_out, lists, counts):
    width = hires.shape[1]
    cols = w_cross_q.shape[1]
    rows = hires.reshape(VIEWS, CH, HEADS, PIECE, width)
    wq = jnp.concatenate([w_cross_q, w_view_qkv.reshape(width, 3 * cols)], axis=1)
    permuted = (lists // 2) % NZ * 8 + (lists // 16) * 2 + lists % 2
    meta = jnp.concatenate(
        [lists.reshape(VIEWS, CH * MAXB), permuted.reshape(VIEWS, CH * MAXB), counts.reshape(VIEWS, CH)], axis=1
    )
    meta = jnp.pad(meta[:, None, :], ((0, 0), (0, 7), (0, HD - 2 * CH * MAXB - CH)))
    vmem = pl.BlockSpec(memory_space=pltpu.VMEM)
    hbm = pl.BlockSpec(memory_space=pl.ANY)
    dma = pltpu.SemaphoreType.DMA
    out = pl.pallas_call(
        kernel,
        out_shape=jax.ShapeDtypeStruct((VIEWS, CH, HD, HD), BF16),
        in_specs=[hbm, hbm, vmem, vmem, vmem, vmem, vmem],
        out_specs=hbm,
        scratch_shapes=[
            pltpu.VMEM((CH, HEADS, VIEWS, PIECE, width), BF16),
            pltpu.VMEM((64, KV_MAIN, 2 * HD), BF16),
            pltpu.VMEM((64, HD - KV_MAIN, 2 * HD), BF16),
            pltpu.VMEM((CH, HEADS, VIEWS, PIECE, 4 * HD), BF16),
            pltpu.VMEM((CH, VIEWS, HD, 2 * HD), BF16),
            pltpu.VMEM((CH, 2, 2, NY, 512, HD), BF16),
            pltpu.VMEM((CH, 2, NY, 512, HD), BF16),
            pltpu.VMEM((CH, 2, 256, HD), BF16),
            pltpu.VMEM((CH, 2, 256, HD), BF16),
            pltpu.VMEM((CH, 2, 512, HD), BF16),
            pltpu.VMEM((CH, 2, 512, HD), BF16),
            pltpu.VMEM((CH, VIEWS, HD, HD), BF16),
            pltpu.VMEM((VIEWS, 8, HD), jnp.int32),
            pltpu.SMEM((VIEWS, 8, HD), jnp.int32),
            dma((CH, 2)), dma((CH, 2)), dma((CH,)),
            dma((CH, 2, 7)), dma((CH, 2, 7)),
            dma((8,)), dma((8,)),
            dma((8, 2)), dma((8, 2)),
            dma((8, 2)), dma((8, 2)),
            dma((4,)), dma((4,)), dma((8,)), dma((8,)),
            dma((CH, 2, 5)), dma((CH, 2, 5)),
            dma((CH, 2)), dma((CH, 2)), dma((CH,)),
            dma, dma, dma,
        ],
        name="upscaler",
        compiler_params=pltpu.CompilerParams(
            collective_id=0, has_side_effects=True, vmem_limit_bytes=60 * 1024 * 1024
        ),
    )(rows, meta, low, gain.reshape(1, width), wq, w_low_kv.reshape(width, 2 * cols), w_out.reshape(2 * cols, width))
    return out.reshape(hires.shape[0], cols)


def solution(mesh):
    in_specs = (
        P("tok", None),
        P("tok", None),
        P(),
        P(None, "head"),
        P(None, None, "head"),
        P(None, None, "head"),
        P(None, "head", None),
        P("tok", None),
        P("tok"),
    )
    return jax.shard_map(shards, mesh=mesh, in_specs=in_specs, out_specs=P("tok", "head"), check_vma=False)
```

```python
import functools
import math

import jax
import jax.numpy as jnp
from jax import lax
from jax.experimental import pallas as pl
from jax.experimental.pallas import tpu as pltpu
from jax.sharding import PartitionSpec as P

HD = 128
VIEWS = 8
MAXB = 8
NY, NZ = 4, 8
CH = 4
PIECE = 16
HEADS = 8
MASKED = -1e30
SCORE_SCALE = math.log2(math.e) / math.sqrt(HD)
MESH = pl.DeviceIdType.MESH
F32 = jnp.float32
BF16 = jnp.bfloat16
Z_ORDER = (0, -1, 1, -2, 2, -3, 3, -4)
SLOT_VIEW = (0, 2, 4, 6, 1, 3, 5, 7)
GROUPS = ((1, 3), (4, 4))
KV_MAIN = 112


def rms_rows(values, gain):
    factor = lax.rsqrt(jnp.mean(values * values, axis=-1, keepdims=True) + 1e-06)
    return (values * factor * gain).astype(BF16)


def dot_t(a, b):
    return lax.dot_general(a, b, (((1,), (1,)), ((), ())), preferred_element_type=F32)


def dot(a, b):
    return jnp.dot(a, b, preferred_element_type=F32)


def kernel(
    x_hbm, lists_hbm, counts_hbm, low_hbm, gain_ref, wcross_hbm, wview_hbm, wlow_hbm, wout_hbm, out_hbm,
    low_ref, wq_ref, wlow_ref, wout_ref,
    xp, kv, kvb, qc, oc, part, pr, fa, fb, r1, r2, res, lists_v, counts_v, lists_s, counts_s,
    s_a, r_a, l_a, s_b, r_b, s_z, r_z, s_x, r_x, s_xf, r_xf, s_h, r_h, s_hz, r_hz,
    s_o, r_o, s_ret, r_ret, l_ret, s_m, r_m, l_m, l_w,
):
    t = lax.axis_index("tok")
    h = lax.axis_index("head")
    x, z = t // NZ, lax.rem(t, NZ)
    y, c = h // 2, lax.rem(h, 2)
    v, q4 = t // 4, lax.rem(t, 4)

    def view_dev(s):
        return {"head": h, "tok": lax.rem(v + s, VIEWS) * 4 + q4}

    def y_of(d):
        return lax.rem(y + d + NY, NY)

    def y_dev(d):
        return {"head": y_of(d) * 2 + c, "tok": t}

    def z_of(d):
        return lax.rem(z + d + NZ, NZ)

    def x_of(d):
        return lax.rem(x + d + 4, 4)

    partner = {"head": y * 2 + 1 - c, "tok": t}
    y_up, y_dn = y_dev(1), y_dev(-1)
    z_up = {"head": h, "tok": x * NZ + z_of(1)}
    z_dn = {"head": h, "tok": x * NZ + z_of(-1)}
    x_up = {"head": h, "tok": x_of(1) * NZ + z}
    x_dn = {"head": h, "tok": x_of(-1) * NZ + z}

    def remote(src, dst, ss, rs, dev):
        return pltpu.make_async_remote_copy(
            src_ref=src, dst_ref=dst, send_sem=ss, recv_sem=rs, device_id=dev, device_id_type=MESH
        )

    def wait_bytes(ref, sem):
        pltpu.make_async_copy(ref, ref, sem).wait()

    loads = [
        pltpu.make_async_copy(low_hbm, low_ref, l_w.at[0]),
        pltpu.make_async_copy(wlow_hbm, wlow_ref, l_w.at[1]),
        pltpu.make_async_copy(wcross_hbm, wq_ref.at[:, pl.ds(0, HD)], l_w.at[2]),
    ]
    for j in range(3):
        loads.append(
            pltpu.make_async_copy(wview_hbm.at[j], wq_ref.at[:, pl.ds((j + 1) * HD, HD)], l_w.at[3 + j])
        )
    loads.append(pltpu.make_async_copy(wout_hbm, wout_ref, l_w.at[6]))
    for load in loads:
        load.start()

    barrier = pltpu.get_barrier_semaphore()
    peers = [view_dev(s) for s in range(1, VIEWS)] + [partner, y_up, y_dn, z_up, z_dn]
    for dev in peers:
        pl.semaphore_signal(barrier, inc=1, device_id=dev, device_id_type=MESH)
    pl.semaphore_wait(barrier, len(peers))

    def slot_of(s):
        return SLOT_VIEW.index(s % VIEWS)

    def slots(g):
        return pl.ds(*GROUPS[g])

    def rows_start(k, g):
        first, n = GROUPS[g]
        for s in SLOT_VIEW[first : first + n]:
            remote(
                x_hbm.at[lax.rem(v + s, VIEWS), k, h], xp.at[k, h, slot_of(-s)],
                s_a.at[k, g], r_a.at[k, g], view_dev(s),
            ).start()
        if g == 0:
            pltpu.make_async_copy(x_hbm.at[v, k], xp.at[k, :, 0], l_a.at[k]).start()

    def piece(k, g, d, other=False):
        return xp.at[k, y_of(d) * 2 + (1 - c if other else c), slots(g)]

    def share(k, g, slot, ref, dev):
        return remote(ref, ref, s_b.at[k, g, slot], r_b.at[k, g, slot], dev)

    def in_a(k, g):
        own = piece(k, g, 0)
        wait_bytes(own, r_a.at[k, g])
        share(k, g, 0, own, y_up).start()
        share(k, g, 1, own, y_dn).start()
        share(k, g, 3, own, partner).start()

    def in_b(k, g):
        wait_bytes(piece(k, g, -1), r_b.at[k, g, 0])
        if g == 0:
            share(k, g, 2, piece(k, g, -1), y_up).start()
        share(k, g, 4, piece(k, g, -1), partner).start()
        wait_bytes(piece(k, g, 1), r_b.at[k, g, 1])
        if g == 1:
            share(k, g, 2, piece(k, g, 1), y_dn).start()
        share(k, g, 5, piece(k, g, 1), partner).start()

    def in_c(k, g):
        wait_bytes(piece(k, g, 2), r_b.at[k, g, 2])
        share(k, g, 6, piece(k, g, 2), partner).start()

    def in_d(k):
        for g in range(2):
            for slot, d in ((3, 0), (4, -1), (5, 1), (6, 2)):
                wait_bytes(piece(k, g, d, True), r_b.at[k, g, slot])
        wait_bytes(xp.at[k, :, 0], l_a.at[k])

    def in_sends(k):
        for g in range(2):
            wait_bytes(piece(k, g, 0), s_a.at[k, g])
            for slot in range(7):
                wait_bytes(piece(k, g, 0), s_b.at[k, g, slot])

    def kv_block(dx, dz):
        return kv.at[pl.ds((x_of(dx) * NZ + z_of(dz)) * 2, 2)]

    def kv_half(dx, dz, part_index):
        return kv.at[(x_of(dx) * NZ + z_of(dz)) * 2 + part_index]

    def kv_z(i, dz, dev):
        return remote(kv_block(0, dz), kv_block(0, dz), s_z.at[i], r_z.at[i], dev)

    def kv_x_start(i):
        ref = kv_block(0, Z_ORDER[i])
        remote(ref, ref, s_x.at[i, 0], r_x.at[i, 0], x_up).start()
        remote(ref, ref, s_x.at[i, 1], r_x.at[i, 1], x_dn).start()

    def kv_x_forward(i):
        dz = Z_ORDER[i]
        wait_bytes(kv_block(-1, dz), r_x.at[i, 0])
        ref = kv_half(-1, dz, 0)
        remote(ref, ref, s_xf.at[i, 0], r_xf.at[i, 0], x_up).start()
        wait_bytes(kv_block(1, dz), r_x.at[i, 1])
        ref = kv_half(1, dz, 1)
        remote(ref, ref, s_xf.at[i, 1], r_xf.at[i, 1], x_dn).start()

    def kv_z_step(i):
        dz = Z_ORDER[i]
        wait_bytes(kv_block(0, dz), r_z.at[i])
        if i + 2 < VIEWS:
            kv_z(i + 2, dz, z_up if dz < 0 else z_dn).start()
        kv_x_start(i)

    def kvb_x_block(d):
        return kvb.at[pl.ds((z * 4 + x_of(d)) * 2, 2)]

    def kvb_x_half(d, e):
        return kvb.at[(z * 4 + x_of(d)) * 2 + e]

    def kvb_z_block(d):
        return kvb.at[pl.ds(z_of(d) * 8, 8)]

    def kvb_x():
        wait_bytes(kvb_x_block(-1), r_h.at[0])
        remote(kvb_x_half(-1, 0), kvb_x_half(-1, 0), s_h.at[2], r_h.at[2], x_up).start()
        wait_bytes(kvb_x_block(1), r_h.at[1])
        remote(kvb_x_half(1, 1), kvb_x_half(1, 1), s_h.at[3], r_h.at[3], x_dn).start()

    def kvb_z(i, dz, dev):
        return remote(kvb_z_block(dz), kvb_z_block(dz), s_hz.at[i], r_hz.at[i], dev)

    def kvb_xf():
        wait_bytes(kvb_x_half(2, 0), r_h.at[2])
        wait_bytes(kvb_x_half(2, 1), r_h.at[3])
        kvb_z(1, 0, z_up).start()
        kvb_z(2, 0, z_dn).start()

    def kvb_z_step(i):
        dz = Z_ORDER[i]
        wait_bytes(kvb_z_block(dz), r_hz.at[i])
        kvb_z(i + 2, dz, z_up if dz < 0 else z_dn).start()

    def kv_last():
        lists_in()
        for i in (6, 7):
            wait_bytes(kvb_z_block(Z_ORDER[i]), r_hz.at[i])
        for i, dz in enumerate(Z_ORDER):
            wait_bytes(kv_half(2, dz, 0), r_xf.at[i, 0])
            wait_bytes(kv_half(2, dz, 1), r_xf.at[i, 1])

    def kv_sends():
        for e in range(2):
            wait_bytes(kvb_x_block(0), s_h.at[e])
            wait_bytes(kvb_x_half(0, e), s_h.at[2 + e])
        for i in range(1, VIEWS):
            wait_bytes(kvb_z_block(0), s_hz.at[i])
        for i, dz in enumerate(Z_ORDER):
            if i:
                wait_bytes(kv_block(0, dz), s_z.at[i])
            for e in range(2):
                wait_bytes(kv_block(0, dz), s_x.at[i, e])
                wait_bytes(kv_half(0, dz, 0), s_xf.at[i, e])

    def lists_start():
        for s in range(1, VIEWS):
            for e, src, dst in ((0, lists_hbm, lists_v), (1, counts_hbm, counts_v)):
                remote(src, dst.at[slot_of(-s)], s_m.at[e], r_m.at[e], view_dev(s)).start()
        pltpu.make_async_copy(lists_hbm, lists_v.at[0], l_m.at[0]).start()
        pltpu.make_async_copy(counts_hbm, counts_v.at[0], l_m.at[1]).start()

    def low_start():
        loads[0].wait()
        loads[1].wait()
        low = rms_rows(low_ref[...].astype(F32), gain_ref[...])
        both = dot(low, wlow_ref[...]).astype(BF16).reshape(2, HD, 2 * HD)
        kv[pl.ds(t * 2, 2)] = both[:, :KV_MAIN]
        kvb[pl.ds((z * 4 + x) * 2, 2)] = both[:, KV_MAIN:]
        kv_z(1, 0, z_up).start()
        kv_z(2, 0, z_dn).start()
        for e, dev in ((0, x_up), (1, x_dn)):
            remote(kvb_x_block(0), kvb_x_block(0), s_h.at[e], r_h.at[e], dev).start()
        kv_x_start(0)

    row = lax.broadcasted_iota(jnp.int32, (HD, HD), 0)
    col = lax.broadcasted_iota(jnp.int32, (HD, HD), 1)
    same_pixel = jnp.where(lax.rem(row, PIECE) == lax.rem(col, PIECE), 0.0, MASKED).astype(F32)

    def project(k):
        def body(r, carry):
            rows = xp[k, pl.ds(r * 2, 2)].reshape(2 * HD, HEADS * HD).astype(F32)
            both = dot(rms_rows(rows, gain_ref[...]), wq_ref[...])
            scaled = jnp.concatenate([both[:, : 2 * HD] * SCORE_SCALE, both[:, 2 * HD :]], axis=1)
            qc[k, pl.ds(r * 2, 2)] = scaled.astype(BF16).reshape(2, VIEWS, PIECE, 4 * HD)
            return carry

        lax.fori_loop(0, HEADS // 2, body, 0)

    def view_attend(k):
        def body(g, carry):
            rows = qc[k, g].reshape(HD, 4 * HD)
            scores = dot_t(rows[:, HD : 2 * HD], rows[:, 2 * HD : 3 * HD]) + same_pixel
            weights = jnp.exp2(scores - jnp.max(scores, axis=-1, keepdims=True))
            total = jnp.sum(weights, axis=-1, keepdims=True)
            mixed = dot(weights.astype(BF16), rows[:, 3 * HD :]) / total
            oc[k, :, pl.ds(g * PIECE, PIECE), HD:] = mixed.astype(BF16).reshape(VIEWS, PIECE, HD)
            return carry

        lax.fori_loop(0, HEADS, body, 0, unroll=4)

    def cross_attend(k, u):
        def body(i, carry):
            s = u * 4 + i
            queries = qc[k, :, s, :, :HD].reshape(HD, HD)
            query_block = v * CH + k
            count = counts_s[s, 0, query_block]
            scores, values = [], []
            for pair in range(MAXB // 2):
                blocks = []
                for e in range(2):
                    block = lists_s[s, 2 * pair + e, query_block]
                    by_z = (lax.rem(block // 2, NZ) * 4 + block // (2 * NZ)) * 2 + lax.rem(block, 2)
                    blocks += [kv[block], kvb[by_z]]
                both = jnp.concatenate(blocks, axis=0)
                keys = both[:, :HD]
                values.append(both[:, HD:])
                raw = dot_t(queries, keys)
                for e in range(2):
                    bias = jnp.where(2 * pair + e < count, 0.0, MASKED).astype(F32)
                    scores.append(raw[:, e * HD : (e + 1) * HD] + bias)
            top = functools.reduce(jnp.maximum, scores)
            top = jnp.max(top, axis=-1, keepdims=True)
            weights = [jnp.exp2(score - top) for score in scores]
            total = jnp.sum(functools.reduce(jnp.add, weights), axis=-1, keepdims=True)
            mixed = functools.reduce(
                jnp.add,
                [
                    dot(jnp.concatenate(weights[2 * p : 2 * p + 2], axis=1).astype(BF16), values[p])
                    for p in range(MAXB // 2)
                ],
            )
            oc[k, s, :, :HD] = (mixed / total).astype(BF16)
            return carry

        lax.fori_loop(0, 4, body, 0, unroll=4)

    def out_project(k, u):
        def body(r, carry):
            rows = oc[k, pl.ds(u * 4 + r * 2, 2)].reshape(2 * HD, 2 * HD)
            summed = dot(rows, wout_ref[...]).astype(BF16)
            for j in range(HEADS):
                part[k, u, j % 2, j // 2, pl.ds(r * 2 * HD, 2 * HD)] = summed[:, j * HD : (j + 1) * HD]
            return carry

        lax.fori_loop(0, 2, body, 0)
        core_send(k, u).start()

    def core_send(k, u):
        return remote(part.at[k, u, 1 - c], pr.at[k, u], s_o.at[k, u, 0], r_o.at[k, u, 0], partner)

    def far_sends(k, u):
        a = y_of(2)
        return (
            remote(part.at[k, u, c, a, pl.ds(0, 256)], fa.at[k, u], s_o.at[k, u, 1], r_o.at[k, u, 1], y_up),
            remote(part.at[k, u, c, a, pl.ds(256, 256)], fb.at[k, u], s_o.at[k, u, 2], r_o.at[k, u, 2], y_dn),
        )

    def near_sends(k, u):
        return (
            remote(part.at[k, u, c, y_of(1)], r1.at[k, u], s_o.at[k, u, 3], r_o.at[k, u, 3], y_up),
            remote(part.at[k, u, c, y_of(-1)], r2.at[k, u], s_o.at[k, u, 4], r_o.at[k, u, 4], y_dn),
        )

    def add_core(k, u, a, rows):
        return part[k, u, c, a, rows].astype(F32) + pr[k, u, a, rows].astype(F32)

    def out_a(k, u):
        core_send(k, u).wait_recv()
        a = y_of(2)

        def body(r, carry):
            rows = pl.ds(r * 256, 256)
            part[k, u, c, a, rows] = add_core(k, u, a, rows).astype(BF16)
            return carry

        lax.fori_loop(0, 2, body, 0)
        for copy in far_sends(k, u):
            copy.start()

    def out_b(k, u):
        for copy in far_sends(k, u):
            copy.wait_recv()
        up, dn = y_of(1), y_of(-1)

        def body(r, carry):
            w, first, second = pl.ds(r * 128, 128), pl.ds(r * 128, 128), pl.ds(256 + r * 128, 128)
            for a, far, with_far, without in ((up, fa, first, second), (dn, fb, second, first)):
                part[k, u, c, a, with_far] = (add_core(k, u, a, with_far) + far[k, u, w].astype(F32)).astype(BF16)
                part[k, u, c, a, without] = add_core(k, u, a, without).astype(BF16)
            return carry

        lax.fori_loop(0, 2, body, 0)
        for copy in near_sends(k, u):
            copy.start()

    def home_slots(u):
        return range(1, 4) if u == 0 else range(4, VIEWS)

    def home(k, u, p):
        return remote(
            res.at[k, p], out_hbm.at[v, k], s_ret.at[k, u], r_ret.at[k, u], view_dev(SLOT_VIEW[p])
        )

    def out_c(k, u):
        for copy in near_sends(k, u):
            copy.wait_recv()

        def body(i, carry):
            p = u * 4 + i
            rows = pl.ds(i * HD, HD)
            total = add_core(k, u, y, rows) + r1[k, u, rows].astype(F32) + r2[k, u, rows].astype(F32)
            columns = pl.ds(pl.multiple_of(h * HD, HD), HD)
            residual = xp[k, :, p, :, columns].reshape(HD, HD).astype(F32)
            res[k, p] = (residual + total).astype(BF16)
            return carry

        lax.fori_loop(0, 4, body, 0)
        for p in home_slots(u):
            home(k, u, p).start()
        if u == 0:
            pltpu.make_async_copy(res.at[k, 0], out_hbm.at[v, k], l_ret.at[k]).start()

    def out_sends(k):
        for u in range(2):
            for copy in (core_send(k, u),) + far_sends(k, u) + near_sends(k, u):
                copy.wait_send()
            sent = res.at[k, slots(u)]
            wait_bytes(sent, s_ret.at[k, u])
            wait_bytes(sent, r_ret.at[k, u])
        wait_bytes(res.at[k, 0], l_ret.at[k])

    def lists_in():
        copies = []
        for e, rows, scalars in ((0, lists_v, lists_s), (1, counts_v, counts_s)):
            wait_bytes(rows.at[pl.ds(1, VIEWS - 1)], r_m.at[e])
            wait_bytes(rows.at[0], l_m.at[e])
            copies.append(pltpu.make_async_copy(rows, scalars, l_m.at[e]))
            copies[e].start()
        for copy in copies:
            copy.wait()

    rows_start(0, 1)
    rows_start(3, 0)
    rows_start(2, 0)
    rows_start(0, 0)
    low_start()
    in_a(2, 0)
    in_a(3, 0)
    lists_start()
    kvb_x()
    rows_start(2, 1)
    in_a(0, 1)
    rows_start(1, 0)
    kv_z_step(1)
    kv_z_step(2)
    kvb_xf()
    kv_x_forward(0)
    in_a(0, 0)
    rows_start(3, 1)
    in_b(2, 0)
    in_b(0, 1)
    in_a(2, 1)
    kv_z_step(3)
    kv_x_forward(1)
    in_c(0, 1)
    in_a(1, 0)
    kv_x_forward(2)
    in_b(2, 1)
    in_b(0, 0)
    kvb_z_step(1)
    kv_z_step(4)
    kvb_z_step(2)
    in_b(3, 0)
    kv_x_forward(3)
    in_a(3, 1)
    kv_z_step(5)
    in_c(2, 1)
    kv_z_step(6)
    in_c(2, 0)
    rows_start(1, 1)
    kv_x_forward(4)
    in_c(0, 0)
    for load in loads[2:]:
        load.wait()
    in_d(2)
    project(2)
    kv_z_step(7)
    in_b(3, 1)
    kvb_z_step(3)
    in_b(1, 0)
    view_attend(2)
    kvb_z_step(4)
    kv_x_forward(5)
    in_c(3, 1)
    kv_x_forward(6)
    in_d(0)
    project(0)
    in_c(3, 0)
    kv_x_forward(7)
    in_c(1, 0)
    kvb_z_step(5)
    in_a(1, 1)
    view_attend(0)
    in_d(3)
    project(3)
    kv_last()
    cross_attend(2, 0)
    out_project(2, 0)
    in_b(1, 1)
    cross_attend(0, 1)
    out_project(0, 1)
    view_attend(3)
    out_a(2, 0)
    cross_attend(2, 1)
    out_a(0, 1)
    out_project(2, 1)
    cross_attend(3, 1)
    out_b(2, 0)
    in_c(1, 1)
    out_project(3, 1)
    out_a(2, 1)
    out_b(0, 1)
    in_d(1)
    project(1)
    view_attend(1)
    out_a(3, 1)
    cross_attend(1, 0)
    cross_attend(3, 0)
    out_b(2, 1)
    out_project(3, 0)
    out_c(0, 1)
    cross_attend(0, 0)
    out_b(3, 1)
    out_project(1, 0)
    out_a(3, 0)
    out_project(0, 0)
    cross_attend(1, 1)
    out_a(1, 0)
    out_project(1, 1)
    out_c(2, 1)
    out_c(3, 1)
    out_a(0, 0)
    out_c(2, 0)
    out_a(1, 1)
    out_b(1, 0)
    out_b(1, 1)
    out_b(0, 0)
    out_b(3, 0)
    out_c(1, 0)
    out_c(1, 1)
    out_c(0, 0)
    out_c(3, 0)

    wait_bytes(lists_v.at[pl.ds(1, VIEWS - 1)], s_m.at[0])
    wait_bytes(counts_v.at[pl.ds(1, VIEWS - 1)], s_m.at[1])
    kv_sends()

    def drain(k, carry):
        in_sends(k)
        out_sends(k)
        return carry

    lax.fori_loop(0, CH, drain, 0)


def shards(hires, low, gain, w_cross_q, w_low_kv, w_view_qkv, w_out, lists, counts):
    width = hires.shape[1]
    cols = w_cross_q.shape[1]
    rows = hires.reshape(VIEWS, CH, HEADS, PIECE, width)
    vmem = pl.BlockSpec(memory_space=pltpu.VMEM)
    hbm = pl.BlockSpec(memory_space=pl.ANY)
    dma = pltpu.SemaphoreType.DMA
    out = pl.pallas_call(
        kernel,
        out_shape=jax.ShapeDtypeStruct((VIEWS, CH, HD, HD), BF16),
        in_specs=[hbm, hbm, hbm, hbm, vmem, hbm, hbm, hbm, hbm],
        out_specs=hbm,
        scratch_shapes=[
            pltpu.VMEM(low.shape, BF16),
            pltpu.VMEM((width, 4 * cols), BF16),
            pltpu.VMEM((width, 2 * cols), BF16),
            pltpu.VMEM((2 * cols, width), BF16),
            pltpu.VMEM((CH, HEADS, VIEWS, PIECE, width), BF16),
            pltpu.VMEM((64, KV_MAIN, 2 * HD), BF16),
            pltpu.VMEM((64, HD - KV_MAIN, 2 * HD), BF16),
            pltpu.VMEM((CH, HEADS, VIEWS, PIECE, 4 * HD), BF16),
            pltpu.VMEM((CH, VIEWS, HD, 2 * HD), BF16),
            pltpu.VMEM((CH, 2, 2, NY, 512, HD), BF16),
            pltpu.VMEM((CH, 2, NY, 512, HD), BF16),
            pltpu.VMEM((CH, 2, 256, HD), BF16),
            pltpu.VMEM((CH, 2, 256, HD), BF16),
            pltpu.VMEM((CH, 2, 512, HD), BF16),
            pltpu.VMEM((CH, 2, 512, HD), BF16),
            pltpu.VMEM((CH, VIEWS, HD, HD), BF16),
            pltpu.VMEM((VIEWS, MAXB, 32), jnp.int32),
            pltpu.VMEM((VIEWS, 1, 32), jnp.int32),
            pltpu.SMEM((VIEWS, MAXB, 32), jnp.int32),
            pltpu.SMEM((VIEWS, 1, 32), jnp.int32),
            dma((CH, 2)), dma((CH, 2)), dma((CH,)),
            dma((CH, 2, 7)), dma((CH, 2, 7)),
            dma((8,)), dma((8,)),
            dma((8, 2)), dma((8, 2)),
            dma((8, 2)), dma((8, 2)),
            dma((4,)), dma((4,)), dma((8,)), dma((8,)),
            dma((CH, 2, 5)), dma((CH, 2, 5)),
            dma((CH, 2)), dma((CH, 2)), dma((CH,)),
            dma((2,)), dma((2,)), dma((2,)), dma((7,)),
        ],
        name="upscaler",
        compiler_params=pltpu.CompilerParams(
            collective_id=0, has_side_effects=True, vmem_limit_bytes=60 * 1024 * 1024
        ),
    )(
        rows, lists.T, counts[None, :], low, gain.reshape(1, width), w_cross_q,
        w_view_qkv.transpose(1, 0, 2), w_low_kv.reshape(width, 2 * cols), w_out.reshape(2 * cols, width),
    )
    return out.reshape(hires.shape[0], cols)


def solution(mesh):
    in_specs = (
        P("tok", None),
        P("tok", None),
        P(),
        P(None, "head"),
        P(None, None, "head"),
        P(None, None, "head"),
        P(None, "head", None),
        P("tok", None),
        P("tok"),
    )
    return jax.shard_map(shards, mesh=mesh, in_specs=in_specs, out_specs=P("tok", "head"), check_vma=False)
```

```python
import functools
import math

import jax
import jax.numpy as jnp
from jax import lax
from jax.experimental import pallas as pl
from jax.experimental.pallas import tpu as pltpu
from jax.sharding import PartitionSpec as P

HD = 128
VIEWS = 8
MAXB = 8
NY, NZ = 4, 8
CH = 4
PIECE = 16
HEADS = 8
MASKED = -1e30
SCORE_SCALE = math.log2(math.e) / math.sqrt(HD)
MESH = pl.DeviceIdType.MESH
F32 = jnp.float32
BF16 = jnp.bfloat16
Z_ORDER = (0, -1, 1, -2, 2, -3, 3, -4)
SLOT_VIEW = (0, 2, 4, 6, 1, 3, 5, 7)
GROUPS = ((1, 3), (4, 4))
KV_MAIN = 112


def rms_rows(values, gain):
    factor = lax.rsqrt(jnp.mean(values * values, axis=-1, keepdims=True) + 1e-06)
    return (values * factor * gain).astype(BF16)


def dot_t(a, b):
    return lax.dot_general(a, b, (((1,), (1,)), ((), ())), preferred_element_type=F32)


def dot(a, b):
    return jnp.dot(a, b, preferred_element_type=F32)


def kernel(
    x_hbm, lists_hbm, counts_hbm, low_hbm, gain_ref, wcross_hbm, wview_hbm, wlow_hbm, wout_hbm, out_hbm,
    low_ref, wq_ref, wlow_ref, wlow_f32, wout_ref,
    xp, kv, kvb, qc, oc, part, pr, fa, fb, r1, r2, res, lists_v, counts_v, lists_s, counts_s,
    s_a, r_a, l_a, s_b, r_b, s_z, r_z, s_x, r_x, s_xf, r_xf, s_h, r_h, s_hz, r_hz,
    s_o, r_o, s_ret, r_ret, l_ret, s_m, r_m, l_m, l_w,
):
    t = lax.axis_index("tok")
    h = lax.axis_index("head")
    x, z = t // NZ, lax.rem(t, NZ)
    y, c = h // 2, lax.rem(h, 2)
    v, q4 = t // 4, lax.rem(t, 4)

    def view_dev(s):
        return {"head": h, "tok": lax.rem(v + s, VIEWS) * 4 + q4}

    def y_of(d):
        return lax.rem(y + d + NY, NY)

    def y_dev(d):
        return {"head": y_of(d) * 2 + c, "tok": t}

    def z_of(d):
        return lax.rem(z + d + NZ, NZ)

    def x_of(d):
        return lax.rem(x + d + 4, 4)

    partner = {"head": y * 2 + 1 - c, "tok": t}
    y_up, y_dn = y_dev(1), y_dev(-1)
    z_up = {"head": h, "tok": x * NZ + z_of(1)}
    z_dn = {"head": h, "tok": x * NZ + z_of(-1)}
    x_up = {"head": h, "tok": x_of(1) * NZ + z}
    x_dn = {"head": h, "tok": x_of(-1) * NZ + z}

    def remote(src, dst, ss, rs, dev):
        return pltpu.make_async_remote_copy(
            src_ref=src, dst_ref=dst, send_sem=ss, recv_sem=rs, device_id=dev, device_id_type=MESH
        )

    def wait_bytes(ref, sem):
        pltpu.make_async_copy(ref, ref, sem).wait()

    loads = [
        pltpu.make_async_copy(low_hbm, low_ref, l_w.at[0]),
        pltpu.make_async_copy(wlow_hbm, wlow_ref, l_w.at[1]),
        pltpu.make_async_copy(wcross_hbm, wq_ref.at[:, pl.ds(0, HD)], l_w.at[2]),
    ]
    for j in range(3):
        loads.append(
            pltpu.make_async_copy(wview_hbm.at[j], wq_ref.at[:, pl.ds((j + 1) * HD, HD)], l_w.at[3 + j])
        )
    loads.append(pltpu.make_async_copy(wout_hbm, wout_ref, l_w.at[6]))
    for load in loads:
        load.start()

    barrier = pltpu.get_barrier_semaphore()
    peers = [view_dev(s) for s in range(1, VIEWS)] + [partner, y_up, y_dn, z_up, z_dn]
    for dev in peers:
        pl.semaphore_signal(barrier, inc=1, device_id=dev, device_id_type=MESH)
    pl.semaphore_wait(barrier, len(peers))

    def slot_of(s):
        return SLOT_VIEW.index(s % VIEWS)

    def slots(g):
        return pl.ds(*GROUPS[g])

    def rows_start(k, g):
        first, n = GROUPS[g]
        for s in SLOT_VIEW[first : first + n]:
            remote(
                x_hbm.at[lax.rem(v + s, VIEWS), k, h], xp.at[k, h, slot_of(-s)],
                s_a.at[k, g], r_a.at[k, g], view_dev(s),
            ).start()
        if g == 0:
            pltpu.make_async_copy(x_hbm.at[v, k], xp.at[k, :, 0], l_a.at[k]).start()

    def piece(k, g, d, other=False):
        return xp.at[k, y_of(d) * 2 + (1 - c if other else c), slots(g)]

    def share(k, g, slot, ref, dev):
        return remote(ref, ref, s_b.at[k, g, slot], r_b.at[k, g, slot], dev)

    def in_a(k, g):
        own = piece(k, g, 0)
        wait_bytes(own, r_a.at[k, g])
        share(k, g, 0, own, y_up).start()
        share(k, g, 1, own, y_dn).start()
        share(k, g, 3, own, partner).start()

    def in_b(k, g):
        wait_bytes(piece(k, g, -1), r_b.at[k, g, 0])
        if g == 0:
            share(k, g, 2, piece(k, g, -1), y_up).start()
        share(k, g, 4, piece(k, g, -1), partner).start()
        wait_bytes(piece(k, g, 1), r_b.at[k, g, 1])
        if g == 1:
            share(k, g, 2, piece(k, g, 1), y_dn).start()
        share(k, g, 5, piece(k, g, 1), partner).start()

    def in_c(k, g):
        wait_bytes(piece(k, g, 2), r_b.at[k, g, 2])
        share(k, g, 6, piece(k, g, 2), partner).start()

    def in_d(k):
        for g in range(2):
            for slot, d in ((3, 0), (4, -1), (5, 1), (6, 2)):
                wait_bytes(piece(k, g, d, True), r_b.at[k, g, slot])
        wait_bytes(xp.at[k, :, 0], l_a.at[k])

    def in_sends(k):
        for g in range(2):
            wait_bytes(piece(k, g, 0), s_a.at[k, g])
            for slot in range(7):
                wait_bytes(piece(k, g, 0), s_b.at[k, g, slot])

    def kv_block(dx, dz):
        return kv.at[pl.ds((x_of(dx) * NZ + z_of(dz)) * 2, 2)]

    def kv_half(dx, dz, part_index):
        return kv.at[(x_of(dx) * NZ + z_of(dz)) * 2 + part_index]

    def kv_z(i, dz, dev):
        return remote(kv_block(0, dz), kv_block(0, dz), s_z.at[i], r_z.at[i], dev)

    def kv_x_start(i):
        ref = kv_block(0, Z_ORDER[i])
        remote(ref, ref, s_x.at[i, 0], r_x.at[i, 0], x_up).start()
        remote(ref, ref, s_x.at[i, 1], r_x.at[i, 1], x_dn).start()

    def kv_x_forward(i):
        dz = Z_ORDER[i]
        wait_bytes(kv_block(-1, dz), r_x.at[i, 0])
        ref = kv_half(-1, dz, 0)
        remote(ref, ref, s_xf.at[i, 0], r_xf.at[i, 0], x_up).start()
        wait_bytes(kv_block(1, dz), r_x.at[i, 1])
        ref = kv_half(1, dz, 1)
        remote(ref, ref, s_xf.at[i, 1], r_xf.at[i, 1], x_dn).start()

    def kv_z_step(i):
        dz = Z_ORDER[i]
        wait_bytes(kv_block(0, dz), r_z.at[i])
        if i + 2 < VIEWS:
            kv_z(i + 2, dz, z_up if dz < 0 else z_dn).start()
        kv_x_start(i)

    def kvb_x_block(d):
        return kvb.at[pl.ds((z * 4 + x_of(d)) * 2, 2)]

    def kvb_x_half(d, e):
        return kvb.at[(z * 4 + x_of(d)) * 2 + e]

    def kvb_z_block(d):
        return kvb.at[pl.ds(z_of(d) * 8, 8)]

    def kvb_x():
        wait_bytes(kvb_x_block(-1), r_h.at[0])
        remote(kvb_x_half(-1, 0), kvb_x_half(-1, 0), s_h.at[2], r_h.at[2], x_up).start()
        wait_bytes(kvb_x_block(1), r_h.at[1])
        remote(kvb_x_half(1, 1), kvb_x_half(1, 1), s_h.at[3], r_h.at[3], x_dn).start()

    def kvb_z(i, dz, dev):
        return remote(kvb_z_block(dz), kvb_z_block(dz), s_hz.at[i], r_hz.at[i], dev)

    def kvb_xf():
        wait_bytes(kvb_x_half(2, 0), r_h.at[2])
        wait_bytes(kvb_x_half(2, 1), r_h.at[3])
        kvb_z(1, 0, z_up).start()
        kvb_z(2, 0, z_dn).start()

    def kvb_z_step(i):
        dz = Z_ORDER[i]
        wait_bytes(kvb_z_block(dz), r_hz.at[i])
        kvb_z(i + 2, dz, z_up if dz < 0 else z_dn).start()

    def kv_last():
        lists_in()
        for i in (6, 7):
            wait_bytes(kvb_z_block(Z_ORDER[i]), r_hz.at[i])
        for i, dz in enumerate(Z_ORDER):
            wait_bytes(kv_half(2, dz, 0), r_xf.at[i, 0])
            wait_bytes(kv_half(2, dz, 1), r_xf.at[i, 1])

    def kv_sends():
        for e in range(2):
            wait_bytes(kvb_x_block(0), s_h.at[e])
            wait_bytes(kvb_x_half(0, e), s_h.at[2 + e])
        for i in range(1, VIEWS):
            wait_bytes(kvb_z_block(0), s_hz.at[i])
        for i, dz in enumerate(Z_ORDER):
            if i:
                wait_bytes(kv_block(0, dz), s_z.at[i])
            for e in range(2):
                wait_bytes(kv_block(0, dz), s_x.at[i, e])
                wait_bytes(kv_half(0, dz, 0), s_xf.at[i, e])

    def lists_start():
        for s in range(1, VIEWS):
            for e, src, dst in ((0, lists_hbm, lists_v), (1, counts_hbm, counts_v)):
                remote(src, dst.at[slot_of(-s)], s_m.at[e], r_m.at[e], view_dev(s)).start()
        pltpu.make_async_copy(lists_hbm, lists_v.at[0], l_m.at[0]).start()
        pltpu.make_async_copy(counts_hbm, counts_v.at[0], l_m.at[1]).start()

    def low_start():
        loads[0].wait()
        loads[1].wait()
        wlow_f32[...] = wlow_ref[...].astype(F32)
        width = low_ref.shape[1]
        both = [wlow_f32[pl.ds(j, width, stride=2), :].astype(BF16) for j in range(2)]
        wlow = jnp.concatenate(both, axis=1)
        low = rms_rows(low_ref[...].astype(F32), gain_ref[...])
        both = dot(low, wlow).astype(BF16).reshape(2, HD, 2 * HD)
        kv[pl.ds(t * 2, 2)] = both[:, :KV_MAIN]
        kvb[pl.ds((z * 4 + x) * 2, 2)] = both[:, KV_MAIN:]
        kv_z(1, 0, z_up).start()
        kv_z(2, 0, z_dn).start()
        for e, dev in ((0, x_up), (1, x_dn)):
            remote(kvb_x_block(0), kvb_x_block(0), s_h.at[e], r_h.at[e], dev).start()
        kv_x_start(0)

    row = lax.broadcasted_iota(jnp.int32, (HD, HD), 0)
    col = lax.broadcasted_iota(jnp.int32, (HD, HD), 1)
    same_pixel = jnp.where(lax.rem(row, PIECE) == lax.rem(col, PIECE), 0.0, MASKED).astype(F32)

    def project(k):
        def body(r, carry):
            rows = xp[k, pl.ds(r * 2, 2)].reshape(2 * HD, HEADS * HD).astype(F32)
            both = dot(rms_rows(rows, gain_ref[...]), wq_ref[...])
            scaled = jnp.concatenate([both[:, : 2 * HD] * SCORE_SCALE, both[:, 2 * HD :]], axis=1)
            qc[k, pl.ds(r * 2, 2)] = scaled.astype(BF16).reshape(2, VIEWS, PIECE, 4 * HD)
            return carry

        lax.fori_loop(0, HEADS // 2, body, 0)

    def view_attend(k):
        def body(g, carry):
            rows = qc[k, g].reshape(HD, 4 * HD)
            scores = dot_t(rows[:, HD : 2 * HD], rows[:, 2 * HD : 3 * HD]) + same_pixel
            weights = jnp.exp2(scores - jnp.max(scores, axis=-1, keepdims=True))
            total = jnp.sum(weights, axis=-1, keepdims=True)
            mixed = dot(weights.astype(BF16), rows[:, 3 * HD :]) / total
            oc[k, :, pl.ds(g * PIECE, PIECE), HD:] = mixed.astype(BF16).reshape(VIEWS, PIECE, HD)
            return carry

        lax.fori_loop(0, HEADS, body, 0, unroll=4)

    def cross_attend(k, u):
        def body(i, carry):
            s = u * 4 + i
            queries = qc[k, :, s, :, :HD].reshape(HD, HD)
            query_block = v * CH + k
            count = counts_s[s, 0, query_block]
            scores, values = [], []
            for pair in range(MAXB // 2):
                blocks = []
                for e in range(2):
                    block = lists_s[s, 2 * pair + e, query_block]
                    by_z = (lax.rem(block // 2, NZ) * 4 + block // (2 * NZ)) * 2 + lax.rem(block, 2)
                    blocks += [kv[block], kvb[by_z]]
                both = jnp.concatenate(blocks, axis=0)
                keys = both[:, :HD]
                values.append(both[:, HD:])
                raw = dot_t(queries, keys)
                for e in range(2):
                    bias = jnp.where(2 * pair + e < count, 0.0, MASKED).astype(F32)
                    scores.append(raw[:, e * HD : (e + 1) * HD] + bias)
            top = functools.reduce(jnp.maximum, scores)
            top = jnp.max(top, axis=-1, keepdims=True)
            weights = [jnp.exp2(score - top) for score in scores]
            total = jnp.sum(functools.reduce(jnp.add, weights), axis=-1, keepdims=True)
            mixed = functools.reduce(
                jnp.add,
                [
                    dot(jnp.concatenate(weights[2 * p : 2 * p + 2], axis=1).astype(BF16), values[p])
                    for p in range(MAXB // 2)
                ],
            )
            oc[k, s, :, :HD] = (mixed / total).astype(BF16)
            return carry

        lax.fori_loop(0, 4, body, 0, unroll=4)

    def out_project(k, u):
        def body(r, carry):
            rows = oc[k, pl.ds(u * 4 + r * 2, 2)].reshape(2 * HD, 2 * HD)
            summed = dot(rows, wout_ref[...]).astype(BF16)
            for j in range(HEADS):
                part[k, u, j % 2, j // 2, pl.ds(r * 2 * HD, 2 * HD)] = summed[:, j * HD : (j + 1) * HD]
            return carry

        lax.fori_loop(0, 2, body, 0)
        core_send(k, u).start()

    def core_send(k, u):
        return remote(part.at[k, u, 1 - c], pr.at[k, u], s_o.at[k, u, 0], r_o.at[k, u, 0], partner)

    def far_sends(k, u):
        a = y_of(2)
        return (
            remote(part.at[k, u, c, a, pl.ds(0, 256)], fa.at[k, u], s_o.at[k, u, 1], r_o.at[k, u, 1], y_up),
            remote(part.at[k, u, c, a, pl.ds(256, 256)], fb.at[k, u], s_o.at[k, u, 2], r_o.at[k, u, 2], y_dn),
        )

    def near_sends(k, u):
        return (
            remote(part.at[k, u, c, y_of(1)], r1.at[k, u], s_o.at[k, u, 3], r_o.at[k, u, 3], y_up),
            remote(part.at[k, u, c, y_of(-1)], r2.at[k, u], s_o.at[k, u, 4], r_o.at[k, u, 4], y_dn),
        )

    def add_core(k, u, a, rows):
        return part[k, u, c, a, rows].astype(F32) + pr[k, u, a, rows].astype(F32)

    def out_a(k, u):
        core_send(k, u).wait_recv()
        a = y_of(2)

        def body(r, carry):
            rows = pl.ds(r * 256, 256)
            part[k, u, c, a, rows] = add_core(k, u, a, rows).astype(BF16)
            return carry

        lax.fori_loop(0, 2, body, 0)
        for copy in far_sends(k, u):
            copy.start()

    def out_b(k, u):
        for copy in far_sends(k, u):
            copy.wait_recv()
        up, dn = y_of(1), y_of(-1)

        def body(r, carry):
            w, first, second = pl.ds(r * 128, 128), pl.ds(r * 128, 128), pl.ds(256 + r * 128, 128)
            for a, far, with_far, without in ((up, fa, first, second), (dn, fb, second, first)):
                part[k, u, c, a, with_far] = (add_core(k, u, a, with_far) + far[k, u, w].astype(F32)).astype(BF16)
                part[k, u, c, a, without] = add_core(k, u, a, without).astype(BF16)
            return carry

        lax.fori_loop(0, 2, body, 0)
        for copy in near_sends(k, u):
            copy.start()

    def home_slots(u):
        return range(1, 4) if u == 0 else range(4, VIEWS)

    def home(k, u, p):
        return remote(
            res.at[k, p], out_hbm.at[v, k], s_ret.at[k, u], r_ret.at[k, u], view_dev(SLOT_VIEW[p])
        )

    def out_c(k, u):
        for copy in near_sends(k, u):
            copy.wait_recv()

        def body(i, carry):
            p = u * 4 + i
            rows = pl.ds(i * HD, HD)
            total = add_core(k, u, y, rows) + r1[k, u, rows].astype(F32) + r2[k, u, rows].astype(F32)
            columns = pl.ds(pl.multiple_of(h * HD, HD), HD)
            residual = xp[k, :, p, :, columns].reshape(HD, HD).astype(F32)
            res[k, p] = (residual + total).astype(BF16)
            return carry

        lax.fori_loop(0, 4, body, 0)
        for p in home_slots(u):
            home(k, u, p).start()
        if u == 0:
            pltpu.make_async_copy(res.at[k, 0], out_hbm.at[v, k], l_ret.at[k]).start()

    def out_sends(k):
        for u in range(2):
            for copy in (core_send(k, u),) + far_sends(k, u) + near_sends(k, u):
                copy.wait_send()
            sent = res.at[k, slots(u)]
            wait_bytes(sent, s_ret.at[k, u])
            wait_bytes(sent, r_ret.at[k, u])
        wait_bytes(res.at[k, 0], l_ret.at[k])

    def lists_in():
        copies = []
        for e, rows, scalars in ((0, lists_v, lists_s), (1, counts_v, counts_s)):
            wait_bytes(rows.at[pl.ds(1, VIEWS - 1)], r_m.at[e])
            wait_bytes(rows.at[0], l_m.at[e])
            copies.append(pltpu.make_async_copy(rows, scalars, l_m.at[e]))
            copies[e].start()
        for copy in copies:
            copy.wait()

    rows_start(0, 1)
    rows_start(3, 0)
    rows_start(2, 0)
    rows_start(0, 0)
    low_start()
    in_a(2, 0)
    in_a(3, 0)
    lists_start()
    kvb_x()
    rows_start(2, 1)
    in_a(0, 1)
    rows_start(1, 0)
    kv_z_step(1)
    kv_z_step(2)
    kvb_xf()
    kv_x_forward(0)
    in_a(0, 0)
    rows_start(3, 1)
    in_b(2, 0)
    in_b(0, 1)
    in_a(2, 1)
    kv_z_step(3)
    kv_x_forward(1)
    in_c(0, 1)
    in_a(1, 0)
    kv_x_forward(2)
    in_b(2, 1)
    in_b(0, 0)
    kvb_z_step(1)
    kv_z_step(4)
    kvb_z_step(2)
    in_b(3, 0)
    kv_x_forward(3)
    in_a(3, 1)
    kv_z_step(5)
    in_c(2, 1)
    kv_z_step(6)
    in_c(2, 0)
    rows_start(1, 1)
    kv_x_forward(4)
    in_c(0, 0)
    for load in loads[2:]:
        load.wait()
    in_d(2)
    project(2)
    kv_z_step(7)
    in_b(3, 1)
    kvb_z_step(3)
    in_b(1, 0)
    view_attend(2)
    kvb_z_step(4)
    kv_x_forward(5)
    in_c(3, 1)
    kv_x_forward(6)
    in_d(0)
    project(0)
    in_c(3, 0)
    kv_x_forward(7)
    in_c(1, 0)
    kvb_z_step(5)
    in_a(1, 1)
    view_attend(0)
    in_d(3)
    project(3)
    kv_last()
    cross_attend(2, 0)
    out_project(2, 0)
    in_b(1, 1)
    cross_attend(0, 1)
    out_project(0, 1)
    view_attend(3)
    out_a(2, 0)
    cross_attend(2, 1)
    out_a(0, 1)
    out_project(2, 1)
    cross_attend(3, 1)
    out_b(2, 0)
    in_c(1, 1)
    out_project(3, 1)
    out_a(2, 1)
    out_b(0, 1)
    in_d(1)
    project(1)
    view_attend(1)
    out_a(3, 1)
    cross_attend(1, 0)
    cross_attend(3, 0)
    out_b(2, 1)
    out_project(3, 0)
    out_c(0, 1)
    cross_attend(0, 0)
    out_b(3, 1)
    out_project(1, 0)
    out_a(3, 0)
    out_project(0, 0)
    cross_attend(1, 1)
    out_a(1, 0)
    out_project(1, 1)
    out_c(2, 1)
    out_c(3, 1)
    out_a(0, 0)
    out_c(2, 0)
    out_a(1, 1)
    out_b(1, 0)
    out_b(1, 1)
    out_b(0, 0)
    out_b(3, 0)
    out_c(1, 0)
    out_c(1, 1)
    out_c(0, 0)
    out_c(3, 0)

    wait_bytes(lists_v.at[pl.ds(1, VIEWS - 1)], s_m.at[0])
    wait_bytes(counts_v.at[pl.ds(1, VIEWS - 1)], s_m.at[1])
    kv_sends()

    def drain(k, carry):
        in_sends(k)
        out_sends(k)
        return carry

    lax.fori_loop(0, CH, drain, 0)


def shards(hires, low, gain, w_cross_q, w_low_kv, w_view_qkv, w_out, lists, counts):
    width = hires.shape[1]
    cols = w_cross_q.shape[1]
    rows = hires.reshape(VIEWS, CH, HEADS, PIECE, width)
    vmem = pl.BlockSpec(memory_space=pltpu.VMEM)
    hbm = pl.BlockSpec(memory_space=pl.ANY)
    dma = pltpu.SemaphoreType.DMA
    out = pl.pallas_call(
        kernel,
        out_shape=jax.ShapeDtypeStruct((VIEWS, CH, HD, HD), BF16),
        in_specs=[hbm, hbm, hbm, hbm, vmem, hbm, hbm, hbm, hbm],
        out_specs=hbm,
        scratch_shapes=[
            pltpu.VMEM(low.shape, BF16),
            pltpu.VMEM((width, 4 * cols), BF16),
            pltpu.VMEM((2 * width, cols), BF16),
            pltpu.VMEM((2 * width, cols), F32),
            pltpu.VMEM((2 * cols, width), BF16),
            pltpu.VMEM((CH, HEADS, VIEWS, PIECE, width), BF16),
            pltpu.VMEM((64, KV_MAIN, 2 * HD), BF16),
            pltpu.VMEM((64, HD - KV_MAIN, 2 * HD), BF16),
            pltpu.VMEM((CH, HEADS, VIEWS, PIECE, 4 * HD), BF16),
            pltpu.VMEM((CH, VIEWS, HD, 2 * HD), BF16),
            pltpu.VMEM((CH, 2, 2, NY, 512, HD), BF16),
            pltpu.VMEM((CH, 2, NY, 512, HD), BF16),
            pltpu.VMEM((CH, 2, 256, HD), BF16),
            pltpu.VMEM((CH, 2, 256, HD), BF16),
            pltpu.VMEM((CH, 2, 512, HD), BF16),
            pltpu.VMEM((CH, 2, 512, HD), BF16),
            pltpu.VMEM((CH, VIEWS, HD, HD), BF16),
            pltpu.VMEM((VIEWS, MAXB, 32), jnp.int32),
            pltpu.VMEM((VIEWS, 1, 32), jnp.int32),
            pltpu.SMEM((VIEWS, MAXB, 32), jnp.int32),
            pltpu.SMEM((VIEWS, 1, 32), jnp.int32),
            dma((CH, 2)), dma((CH, 2)), dma((CH,)),
            dma((CH, 2, 7)), dma((CH, 2, 7)),
            dma((8,)), dma((8,)),
            dma((8, 2)), dma((8, 2)),
            dma((8, 2)), dma((8, 2)),
            dma((4,)), dma((4,)), dma((8,)), dma((8,)),
            dma((CH, 2, 5)), dma((CH, 2, 5)),
            dma((CH, 2)), dma((CH, 2)), dma((CH,)),
            dma((2,)), dma((2,)), dma((2,)), dma((7,)),
        ],
        name="upscaler",
        compiler_params=pltpu.CompilerParams(
            collective_id=0, has_side_effects=True, vmem_limit_bytes=60 * 1024 * 1024
        ),
    )(
        rows, lists.T, counts[None, :], low, gain.reshape(1, width), w_cross_q,
        w_view_qkv.transpose(1, 0, 2), w_low_kv.reshape(2 * width, cols), w_out.reshape(2 * cols, width),
    )
    return out.reshape(hires.shape[0], cols)


def solution(mesh):
    in_specs = (
        P("tok", None),
        P("tok", None),
        P(),
        P(None, "head"),
        P(None, None, "head"),
        P(None, None, "head"),
        P(None, "head", None),
        P("tok", None),
        P("tok"),
    )
    return jax.shard_map(shards, mesh=mesh, in_specs=in_specs, out_specs=P("tok", "head"), check_vma=False)
```

```python
import functools
import math

import jax
import jax.numpy as jnp
from jax import lax
from jax.experimental import pallas as pl
from jax.experimental.pallas import tpu as pltpu
from jax.sharding import PartitionSpec as P

HD = 128
VIEWS = 8
MAXB = 8
NY, NZ = 4, 8
CH = 4
PIECE = 16
HEADS = 8
MASKED = -1e30
SCORE_SCALE = math.log2(math.e) / math.sqrt(HD)
MESH = pl.DeviceIdType.MESH
F32 = jnp.float32
BF16 = jnp.bfloat16
Z_ORDER = (0, -1, 1, -2, 2, -3, 3, -4)
SLOT_VIEW = (0, 2, 4, 6, 1, 3, 5, 7)
GROUPS = ((1, 3), (4, 4))
KV_MAIN = 112


def rms_rows(values, gain):
    factor = lax.rsqrt(jnp.mean(values * values, axis=-1, keepdims=True) + 1e-06)
    return (values * factor * gain).astype(BF16)


def dot_t(a, b):
    return lax.dot_general(a, b, (((1,), (1,)), ((), ())), preferred_element_type=F32)


def dot(a, b):
    return jnp.dot(a, b, preferred_element_type=F32)


def kernel(
    x_hbm, lists_hbm, counts_hbm, low_hbm, gain_ref, wcross_hbm, wview_hbm, wlow_hbm, wout_hbm, out_hbm,
    low_ref, wq_ref, wlow_ref, wlow_f32, wout_ref,
    xp, kv, kvb, qc, oc, part, pr, fa, fb, r1, r2, res, lists_v, counts_v, lists_s, counts_s,
    s_a, r_a, l_a, s_b, r_b, s_z, r_z, s_x, r_x, s_xf, r_xf, s_h, r_h, s_hz, r_hz,
    s_o, r_o, s_ret, r_ret, l_ret, s_m, r_m, l_m, l_w,
):
    t = lax.axis_index("tok")
    h = lax.axis_index("head")
    x, z = t // NZ, lax.rem(t, NZ)
    y, c = h // 2, lax.rem(h, 2)
    v, q4 = t // 4, lax.rem(t, 4)

    def view_dev(s):
        return {"head": h, "tok": lax.rem(v + s, VIEWS) * 4 + q4}

    def y_of(d):
        return lax.rem(y + d + NY, NY)

    def y_dev(d):
        return {"head": y_of(d) * 2 + c, "tok": t}

    def z_of(d):
        return lax.rem(z + d + NZ, NZ)

    def x_of(d):
        return lax.rem(x + d + 4, 4)

    partner = {"head": y * 2 + 1 - c, "tok": t}
    y_up, y_dn = y_dev(1), y_dev(-1)
    z_up = {"head": h, "tok": x * NZ + z_of(1)}
    z_dn = {"head": h, "tok": x * NZ + z_of(-1)}
    x_up = {"head": h, "tok": x_of(1) * NZ + z}
    x_dn = {"head": h, "tok": x_of(-1) * NZ + z}

    def remote(src, dst, ss, rs, dev):
        return pltpu.make_async_remote_copy(
            src_ref=src, dst_ref=dst, send_sem=ss, recv_sem=rs, device_id=dev, device_id_type=MESH
        )

    def wait_bytes(ref, sem):
        pltpu.make_async_copy(ref, ref, sem).wait()

    loads = [
        pltpu.make_async_copy(low_hbm, low_ref, l_w.at[0]),
        pltpu.make_async_copy(wlow_hbm, wlow_ref, l_w.at[1]),
        pltpu.make_async_copy(wcross_hbm, wq_ref.at[:, pl.ds(0, HD)], l_w.at[2]),
    ]
    for j in range(3):
        loads.append(
            pltpu.make_async_copy(wview_hbm.at[j], wq_ref.at[:, pl.ds((j + 1) * HD, HD)], l_w.at[3 + j])
        )
    loads.append(pltpu.make_async_copy(wout_hbm, wout_ref, l_w.at[6]))
    for load in loads:
        load.start()

    barrier = pltpu.get_barrier_semaphore()
    peers = [view_dev(s) for s in range(1, VIEWS)] + [partner, y_up, y_dn, z_up, z_dn]
    for dev in peers:
        pl.semaphore_signal(barrier, inc=1, device_id=dev, device_id_type=MESH)
    pl.semaphore_wait(barrier, len(peers))

    def slot_of(s):
        return SLOT_VIEW.index(s % VIEWS)

    def slots(g):
        return pl.ds(*GROUPS[g])

    def rows_start(k, g):
        first, n = GROUPS[g]
        for s in SLOT_VIEW[first : first + n]:
            remote(
                x_hbm.at[lax.rem(v + s, VIEWS), k, h], xp.at[k, h, slot_of(-s)],
                s_a.at[k, g], r_a.at[k, g], view_dev(s),
            ).start()
        if g == 0:
            pltpu.make_async_copy(x_hbm.at[v, k], xp.at[k, :, 0], l_a.at[k]).start()

    def piece(k, g, d, other=False):
        return xp.at[k, y_of(d) * 2 + (1 - c if other else c), slots(g)]

    def share(k, g, slot, ref, dev):
        return remote(ref, ref, s_b.at[k, g, slot], r_b.at[k, g, slot], dev)

    def in_a(k, g):
        own = piece(k, g, 0)
        wait_bytes(own, r_a.at[k, g])
        share(k, g, 0, own, y_up).start()
        share(k, g, 1, own, y_dn).start()
        share(k, g, 3, own, partner).start()

    def in_b(k, g):
        wait_bytes(piece(k, g, -1), r_b.at[k, g, 0])
        if g == 0:
            share(k, g, 2, piece(k, g, -1), y_up).start()
        share(k, g, 4, piece(k, g, -1), partner).start()
        wait_bytes(piece(k, g, 1), r_b.at[k, g, 1])
        if g == 1:
            share(k, g, 2, piece(k, g, 1), y_dn).start()
        share(k, g, 5, piece(k, g, 1), partner).start()

    def in_c(k, g):
        wait_bytes(piece(k, g, 2), r_b.at[k, g, 2])
        share(k, g, 6, piece(k, g, 2), partner).start()

    def in_d(k):
        for g in range(2):
            for slot, d in ((3, 0), (4, -1), (5, 1), (6, 2)):
                wait_bytes(piece(k, g, d, True), r_b.at[k, g, slot])
        wait_bytes(xp.at[k, :, 0], l_a.at[k])

    def in_sends(k):
        for g in range(2):
            wait_bytes(piece(k, g, 0), s_a.at[k, g])
            for slot in range(7):
                wait_bytes(piece(k, g, 0), s_b.at[k, g, slot])

    def kv_block(dx, dz):
        return kv.at[pl.ds((x_of(dx) * NZ + z_of(dz)) * 2, 2)]

    def kv_half(dx, dz, part_index):
        return kv.at[(x_of(dx) * NZ + z_of(dz)) * 2 + part_index]

    def kv_z(i, dz, dev):
        return remote(kv_block(0, dz), kv_block(0, dz), s_z.at[i], r_z.at[i], dev)

    def kv_x_start(i):
        ref = kv_block(0, Z_ORDER[i])
        remote(ref, ref, s_x.at[i, 0], r_x.at[i, 0], x_up).start()
        remote(ref, ref, s_x.at[i, 1], r_x.at[i, 1], x_dn).start()

    def kv_x_forward(i):
        dz = Z_ORDER[i]
        wait_bytes(kv_block(-1, dz), r_x.at[i, 0])
        ref = kv_half(-1, dz, 0)
        remote(ref, ref, s_xf.at[i, 0], r_xf.at[i, 0], x_up).start()
        wait_bytes(kv_block(1, dz), r_x.at[i, 1])
        ref = kv_half(1, dz, 1)
        remote(ref, ref, s_xf.at[i, 1], r_xf.at[i, 1], x_dn).start()

    def kv_z_step(i):
        dz = Z_ORDER[i]
        wait_bytes(kv_block(0, dz), r_z.at[i])
        if i + 2 < VIEWS:
            kv_z(i + 2, dz, z_up if dz < 0 else z_dn).start()
        kv_x_start(i)

    def kvb_x_block(d):
        return kvb.at[pl.ds((z * 4 + x_of(d)) * 2, 2)]

    def kvb_x_half(d, e):
        return kvb.at[(z * 4 + x_of(d)) * 2 + e]

    def kvb_z_block(d):
        return kvb.at[pl.ds(z_of(d) * 8, 8)]

    def kvb_x():
        wait_bytes(kvb_x_block(-1), r_h.at[0])
        remote(kvb_x_half(-1, 0), kvb_x_half(-1, 0), s_h.at[2], r_h.at[2], x_up).start()
        wait_bytes(kvb_x_block(1), r_h.at[1])
        remote(kvb_x_half(1, 1), kvb_x_half(1, 1), s_h.at[3], r_h.at[3], x_dn).start()

    def kvb_z(i, dz, dev):
        return remote(kvb_z_block(dz), kvb_z_block(dz), s_hz.at[i], r_hz.at[i], dev)

    def kvb_xf():
        wait_bytes(kvb_x_half(2, 0), r_h.at[2])
        wait_bytes(kvb_x_half(2, 1), r_h.at[3])
        kvb_z(1, 0, z_up).start()
        kvb_z(2, 0, z_dn).start()

    def kvb_z_step(i):
        dz = Z_ORDER[i]
        wait_bytes(kvb_z_block(dz), r_hz.at[i])
        kvb_z(i + 2, dz, z_up if dz < 0 else z_dn).start()

    def kv_last():
        lists_in()
        for i in (6, 7):
            wait_bytes(kvb_z_block(Z_ORDER[i]), r_hz.at[i])
        for i, dz in enumerate(Z_ORDER):
            wait_bytes(kv_half(2, dz, 0), r_xf.at[i, 0])
            wait_bytes(kv_half(2, dz, 1), r_xf.at[i, 1])

    def kv_sends():
        for e in range(2):
            wait_bytes(kvb_x_block(0), s_h.at[e])
            wait_bytes(kvb_x_half(0, e), s_h.at[2 + e])
        for i in range(1, VIEWS):
            wait_bytes(kvb_z_block(0), s_hz.at[i])
        for i, dz in enumerate(Z_ORDER):
            if i:
                wait_bytes(kv_block(0, dz), s_z.at[i])
            for e in range(2):
                wait_bytes(kv_block(0, dz), s_x.at[i, e])
                wait_bytes(kv_half(0, dz, 0), s_xf.at[i, e])

    def lists_start():
        for s in range(1, VIEWS):
            for e, src, dst in ((0, lists_hbm, lists_v), (1, counts_hbm, counts_v)):
                remote(src, dst.at[slot_of(-s)], s_m.at[e], r_m.at[e], view_dev(s)).start()
        pltpu.make_async_copy(lists_hbm, lists_v.at[0], l_m.at[0]).start()
        pltpu.make_async_copy(counts_hbm, counts_v.at[0], l_m.at[1]).start()

    def low_start():
        loads[0].wait()
        loads[1].wait()
        wlow_f32[...] = wlow_ref[...].astype(F32)
        width = low_ref.shape[1]
        both = [wlow_f32[pl.ds(j, width, stride=2), :].astype(BF16) for j in range(2)]
        wlow = jnp.concatenate(both, axis=1)
        low = rms_rows(low_ref[...].astype(F32), gain_ref[...])
        both = dot(low, wlow).astype(BF16).reshape(2, HD, 2 * HD)
        kv[pl.ds(t * 2, 2)] = both[:, :KV_MAIN]
        kvb[pl.ds((z * 4 + x) * 2, 2)] = both[:, KV_MAIN:]
        kv_z(1, 0, z_up).start()
        kv_z(2, 0, z_dn).start()
        for e, dev in ((0, x_up), (1, x_dn)):
            remote(kvb_x_block(0), kvb_x_block(0), s_h.at[e], r_h.at[e], dev).start()
        kv_x_start(0)

    row = lax.broadcasted_iota(jnp.int32, (HD, HD), 0)
    col = lax.broadcasted_iota(jnp.int32, (HD, HD), 1)
    same_pixel = jnp.where(lax.rem(row, PIECE) == lax.rem(col, PIECE), 0.0, MASKED).astype(F32)

    def project(k):
        def body(r, carry):
            rows = xp[k, pl.ds(r * 2, 2)].reshape(2 * HD, HEADS * HD).astype(F32)
            both = dot(rms_rows(rows, gain_ref[...]), wq_ref[...])
            scaled = jnp.concatenate([both[:, : 2 * HD] * SCORE_SCALE, both[:, 2 * HD :]], axis=1)
            qc[k, pl.ds(r * 2, 2)] = scaled.astype(BF16).reshape(2, VIEWS, PIECE, 4 * HD)
            return carry

        lax.fori_loop(0, HEADS // 2, body, 0)

    def view_attend(k):
        def body(g, carry):
            rows = qc[k, g].reshape(HD, 4 * HD)
            scores = dot_t(rows[:, HD : 2 * HD], rows[:, 2 * HD : 3 * HD]) + same_pixel
            weights = jnp.exp2(scores - jnp.max(scores, axis=-1, keepdims=True))
            total = jnp.sum(weights, axis=-1, keepdims=True)
            mixed = dot(weights.astype(BF16), rows[:, 3 * HD :]) / total
            oc[k, :, pl.ds(g * PIECE, PIECE), HD:] = mixed.astype(BF16).reshape(VIEWS, PIECE, HD)
            return carry

        lax.fori_loop(0, HEADS, body, 0, unroll=4)

    def cross_attend(k, u):
        def body(i, carry):
            s = u * 4 + i
            queries = qc[k, :, s, :, :HD].reshape(HD, HD)
            query_block = v * CH + k
            count = counts_s[s, 0, query_block]
            scores, values = [], []
            for pair in range(MAXB // 2):
                blocks = []
                for e in range(2):
                    block = lists_s[s, 2 * pair + e, query_block]
                    by_z = (lax.rem(block // 2, NZ) * 4 + block // (2 * NZ)) * 2 + lax.rem(block, 2)
                    blocks += [kv[block], kvb[by_z]]
                both = jnp.concatenate(blocks, axis=0)
                keys = both[:, :HD]
                values.append(both[:, HD:])
                raw = dot_t(queries, keys)
                for e in range(2):
                    bias = jnp.where(2 * pair + e < count, 0.0, MASKED).astype(F32)
                    scores.append(raw[:, e * HD : (e + 1) * HD] + bias)
            top = functools.reduce(jnp.maximum, scores)
            top = jnp.max(top, axis=-1, keepdims=True)
            weights = [jnp.exp2(score - top) for score in scores]
            total = jnp.sum(functools.reduce(jnp.add, weights), axis=-1, keepdims=True)
            mixed = functools.reduce(
                jnp.add,
                [
                    dot(jnp.concatenate(weights[2 * p : 2 * p + 2], axis=1).astype(BF16), values[p])
                    for p in range(MAXB // 2)
                ],
            )
            oc[k, s, :, :HD] = (mixed / total).astype(BF16)
            return carry

        lax.fori_loop(0, 4, body, 0, unroll=4)

    def out_project(k, u):
        def body(r, carry):
            rows = oc[k, pl.ds(u * 4 + r * 2, 2)].reshape(2 * HD, 2 * HD)
            summed = dot(rows, wout_ref[...]).astype(BF16)
            for j in range(HEADS):
                part[k, u, j % 2, j // 2, pl.ds(r * 2 * HD, 2 * HD)] = summed[:, j * HD : (j + 1) * HD]
            return carry

        lax.fori_loop(0, 2, body, 0, unroll=2)
        core_send(k, u).start()

    def core_send(k, u):
        return remote(part.at[k, u, 1 - c], pr.at[k, u], s_o.at[k, u, 0], r_o.at[k, u, 0], partner)

    def far_sends(k, u):
        a = y_of(2)
        return (
            remote(part.at[k, u, c, a, pl.ds(0, 256)], fa.at[k, u], s_o.at[k, u, 1], r_o.at[k, u, 1], y_up),
            remote(part.at[k, u, c, a, pl.ds(256, 256)], fb.at[k, u], s_o.at[k, u, 2], r_o.at[k, u, 2], y_dn),
        )

    def near_sends(k, u):
        return (
            remote(part.at[k, u, c, y_of(1)], r1.at[k, u], s_o.at[k, u, 3], r_o.at[k, u, 3], y_up),
            remote(part.at[k, u, c, y_of(-1)], r2.at[k, u], s_o.at[k, u, 4], r_o.at[k, u, 4], y_dn),
        )

    def add_core(k, u, a, rows):
        return part[k, u, c, a, rows].astype(F32) + pr[k, u, a, rows].astype(F32)

    def out_a(k, u):
        core_send(k, u).wait_recv()
        a = y_of(2)

        def body(r, carry):
            rows = pl.ds(r * 256, 256)
            part[k, u, c, a, rows] = add_core(k, u, a, rows).astype(BF16)
            return carry

        lax.fori_loop(0, 2, body, 0, unroll=2)
        for copy in far_sends(k, u):
            copy.start()

    def out_b(k, u):
        for copy in far_sends(k, u):
            copy.wait_recv()
        up, dn = y_of(1), y_of(-1)

        def body(r, carry):
            w, first, second = pl.ds(r * 128, 128), pl.ds(r * 128, 128), pl.ds(256 + r * 128, 128)
            for a, far, with_far, without in ((up, fa, first, second), (dn, fb, second, first)):
                part[k, u, c, a, with_far] = (add_core(k, u, a, with_far) + far[k, u, w].astype(F32)).astype(BF16)
                part[k, u, c, a, without] = add_core(k, u, a, without).astype(BF16)
            return carry

        lax.fori_loop(0, 2, body, 0, unroll=2)
        for copy in near_sends(k, u):
            copy.start()

    def home_slots(u):
        return range(1, 4) if u == 0 else range(4, VIEWS)

    def home(k, u, p):
        return remote(
            res.at[k, p], out_hbm.at[v, k], s_ret.at[k, u], r_ret.at[k, u], view_dev(SLOT_VIEW[p])
        )

    def out_c(k, u):
        for copy in near_sends(k, u):
            copy.wait_recv()

        def body(i, carry):
            p = u * 4 + i
            rows = pl.ds(i * HD, HD)
            total = add_core(k, u, y, rows) + r1[k, u, rows].astype(F32) + r2[k, u, rows].astype(F32)
            columns = pl.ds(pl.multiple_of(h * HD, HD), HD)
            residual = xp[k, :, p, :, columns].reshape(HD, HD).astype(F32)
            res[k, p] = (residual + total).astype(BF16)
            return carry

        lax.fori_loop(0, 4, body, 0, unroll=4)
        for p in home_slots(u):
            home(k, u, p).start()
        if u == 0:
            pltpu.make_async_copy(res.at[k, 0], out_hbm.at[v, k], l_ret.at[k]).start()

    def out_sends(k):
        for u in range(2):
            for copy in (core_send(k, u),) + far_sends(k, u) + near_sends(k, u):
                copy.wait_send()
            sent = res.at[k, slots(u)]
            wait_bytes(sent, s_ret.at[k, u])
            wait_bytes(sent, r_ret.at[k, u])
        wait_bytes(res.at[k, 0], l_ret.at[k])

    def lists_in():
        copies = []
        for e, rows, scalars in ((0, lists_v, lists_s), (1, counts_v, counts_s)):
            wait_bytes(rows.at[pl.ds(1, VIEWS - 1)], r_m.at[e])
            wait_bytes(rows.at[0], l_m.at[e])
            copies.append(pltpu.make_async_copy(rows, scalars, l_m.at[e]))
            copies[e].start()
        for copy in copies:
            copy.wait()

    rows_start(0, 1)
    rows_start(3, 0)
    rows_start(2, 0)
    rows_start(0, 0)
    low_start()
    in_a(2, 0)
    in_a(3, 0)
    lists_start()
    kvb_x()
    rows_start(2, 1)
    in_a(0, 1)
    rows_start(1, 0)
    kv_z_step(1)
    kv_z_step(2)
    kvb_xf()
    kv_x_forward(0)
    in_a(0, 0)
    rows_start(3, 1)
    in_b(2, 0)
    in_b(0, 1)
    in_a(2, 1)
    kv_z_step(3)
    kv_x_forward(1)
    in_c(0, 1)
    in_a(1, 0)
    kv_x_forward(2)
    in_b(2, 1)
    in_b(0, 0)
    kvb_z_step(1)
    kv_z_step(4)
    kvb_z_step(2)
    in_b(3, 0)
    kv_x_forward(3)
    in_a(3, 1)
    kv_z_step(5)
    in_c(2, 1)
    kv_z_step(6)
    in_c(2, 0)
    rows_start(1, 1)
    kv_x_forward(4)
    in_c(0, 0)
    for load in loads[2:]:
        load.wait()
    in_d(2)
    project(2)
    kv_z_step(7)
    in_b(3, 1)
    kvb_z_step(3)
    in_b(1, 0)
    view_attend(2)
    kvb_z_step(4)
    kv_x_forward(5)
    in_c(3, 1)
    kv_x_forward(6)
    in_d(0)
    project(0)
    in_c(3, 0)
    kv_x_forward(7)
    in_c(1, 0)
    kvb_z_step(5)
    in_a(1, 1)
    view_attend(0)
    in_d(3)
    project(3)
    kv_last()
    cross_attend(2, 0)
    out_project(2, 0)
    in_b(1, 1)
    cross_attend(0, 1)
    out_project(0, 1)
    view_attend(3)
    out_a(2, 0)
    cross_attend(2, 1)
    out_a(0, 1)
    out_project(2, 1)
    cross_attend(3, 1)
    out_b(2, 0)
    in_c(1, 1)
    out_project(3, 1)
    out_a(2, 1)
    out_b(0, 1)
    in_d(1)
    project(1)
    view_attend(1)
    out_a(3, 1)
    cross_attend(1, 0)
    cross_attend(3, 0)
    out_b(2, 1)
    out_project(3, 0)
    out_c(0, 1)
    cross_attend(0, 0)
    out_b(3, 1)
    out_project(1, 0)
    out_a(3, 0)
    out_project(0, 0)
    cross_attend(1, 1)
    out_a(1, 0)
    out_project(1, 1)
    out_c(2, 1)
    out_c(3, 1)
    out_a(0, 0)
    out_c(2, 0)
    out_a(1, 1)
    out_b(1, 0)
    out_b(1, 1)
    out_b(0, 0)
    out_b(3, 0)
    out_c(1, 0)
    out_c(1, 1)
    out_c(0, 0)
    out_c(3, 0)

    wait_bytes(lists_v.at[pl.ds(1, VIEWS - 1)], s_m.at[0])
    wait_bytes(counts_v.at[pl.ds(1, VIEWS - 1)], s_m.at[1])
    kv_sends()

    def drain(k, carry):
        in_sends(k)
        out_sends(k)
        return carry

    lax.fori_loop(0, CH, drain, 0)


def shards(hires, low, gain, w_cross_q, w_low_kv, w_view_qkv, w_out, lists, counts):
    width = hires.shape[1]
    cols = w_cross_q.shape[1]
    rows = hires.reshape(VIEWS, CH, HEADS, PIECE, width)
    vmem = pl.BlockSpec(memory_space=pltpu.VMEM)
    hbm = pl.BlockSpec(memory_space=pl.ANY)
    dma = pltpu.SemaphoreType.DMA
    out = pl.pallas_call(
        kernel,
        out_shape=jax.ShapeDtypeStruct((VIEWS, CH, HD, HD), BF16),
        in_specs=[hbm, hbm, hbm, hbm, vmem, hbm, hbm, hbm, hbm],
        out_specs=hbm,
        scratch_shapes=[
            pltpu.VMEM(low.shape, BF16),
            pltpu.VMEM((width, 4 * cols), BF16),
            pltpu.VMEM((2 * width, cols), BF16),
            pltpu.VMEM((2 * width, cols), F32),
            pltpu.VMEM((2 * cols, width), BF16),
            pltpu.VMEM((CH, HEADS, VIEWS, PIECE, width), BF16),
            pltpu.VMEM((64, KV_MAIN, 2 * HD), BF16),
            pltpu.VMEM((64, HD - KV_MAIN, 2 * HD), BF16),
            pltpu.VMEM((CH, HEADS, VIEWS, PIECE, 4 * HD), BF16),
            pltpu.VMEM((CH, VIEWS, HD, 2 * HD), BF16),
            pltpu.VMEM((CH, 2, 2, NY, 512, HD), BF16),
            pltpu.VMEM((CH, 2, NY, 512, HD), BF16),
            pltpu.VMEM((CH, 2, 256, HD), BF16),
            pltpu.VMEM((CH, 2, 256, HD), BF16),
            pltpu.VMEM((CH, 2, 512, HD), BF16),
            pltpu.VMEM((CH, 2, 512, HD), BF16),
            pltpu.VMEM((CH, VIEWS, HD, HD), BF16),
            pltpu.VMEM((VIEWS, MAXB, 32), jnp.int32),
            pltpu.VMEM((VIEWS, 1, 32), jnp.int32),
            pltpu.SMEM((VIEWS, MAXB, 32), jnp.int32),
            pltpu.SMEM((VIEWS, 1, 32), jnp.int32),
            dma((CH, 2)), dma((CH, 2)), dma((CH,)),
            dma((CH, 2, 7)), dma((CH, 2, 7)),
            dma((8,)), dma((8,)),
            dma((8, 2)), dma((8, 2)),
            dma((8, 2)), dma((8, 2)),
            dma((4,)), dma((4,)), dma((8,)), dma((8,)),
            dma((CH, 2, 5)), dma((CH, 2, 5)),
            dma((CH, 2)), dma((CH, 2)), dma((CH,)),
            dma((2,)), dma((2,)), dma((2,)), dma((7,)),
        ],
        name="upscaler",
        compiler_params=pltpu.CompilerParams(
            collective_id=0, has_side_effects=True, vmem_limit_bytes=60 * 1024 * 1024
        ),
    )(
        rows, lists.T, counts[None, :], low, gain.reshape(1, width), w_cross_q,
        w_view_qkv.transpose(1, 0, 2), w_low_kv.reshape(2 * width, cols), w_out.reshape(2 * cols, width),
    )
    return out.reshape(hires.shape[0], cols)


def solution(mesh):
    in_specs = (
        P("tok", None),
        P("tok", None),
        P(),
        P(None, "head"),
        P(None, None, "head"),
        P(None, None, "head"),
        P(None, "head", None),
        P("tok", None),
        P("tok"),
    )
    return jax.shard_map(shards, mesh=mesh, in_specs=in_specs, out_specs=P("tok", "head"), check_vma=False)
```
